512 devices in a mesh: pairs: 128 (over x, z, core), rep: 4 (over y).
Axes of the slice: x: 4, y: 4, z: 16, core: 2. Of those that a mesh axis runs over, the one named last changes fastest.
Arguments:
- positions: float32 [3, 2048, 256], P(None, 'pairs'), may hold values from -1 to 1
- facing: float32 [2, 2048, 256], P(None, 'pairs'), may hold values from -3.140625 to 3.140625
- area: float32 [2048, 256], P('pairs'), may hold values from 0.00390625 to 0.03125
- emission: float32 [2048, 8, 256], P('pairs'), may hold values from 0.1 to 2
- reflect: float32 [2048, 8, 256], P('pairs'), may hold values from 0.2 to 0.9
- pair_list: int32 [128, 4, 128, 1, 2], P('pairs', 'rep'), may hold values from -1 to 2047, as said below
Outputs:
- radiosity: float32 [2048, 8, 256], P('pairs')
The draws below stay inside these ranges and needn't reach their ends.
Inputs may be any that keep to these rules, and one draw needn't show every extreme that they name: `pair_list`: entry [p, r, q, c] is held by the device at pairs index p and rep index r in its slot c toward pairs index q. Its row block lies in p * 16 to (p + 1) * 16 - 1 and its column block in q * 16 to (q + 1) * 16 - 1, or both entries are -1 for an empty slot. Slots toward pairs index 0 are never empty.
All inputs are finite; a program needn't handle non-finite values.
Results may differ from the reference program's by a relative error of at most 0.0003.
Values may be sent and summed in bfloat16 or wider, within the bound.
A program may use at most 64 MiB of HBM per device.

```python
import math
import jax
import jax.numpy as jnp
from jax import lax

P_SIZE = 256
BANDS = 8
BLK_DEV = 16
CAP = 1
SWEEPS = 2
OWNERS = 128
GROUPS = 4
NBLK = 2048


def draw_pair_list(key, part):
    subkeys = jax.random.split(jax.random.fold_in(key, 17), 4)
    grid_shape = (OWNERS, GROUPS, OWNERS, CAP)
    busiest = jax.random.randint(subkeys[0], (OWNERS, 1, 1, 1), 0, GROUPS)
    group_index = jnp.arange(GROUPS, dtype=jnp.int32).reshape(1, GROUPS, 1, 1)
    source_index = jnp.arange(OWNERS, dtype=jnp.int32).reshape(OWNERS, 1, 1, 1)
    target_index = jnp.arange(OWNERS, dtype=jnp.int32).reshape(1, 1, OWNERS, 1)
    threshold = jnp.where(group_index == busiest, 19, 5)
    active = (jax.random.randint(subkeys[1], grid_shape, 0, 20) < threshold) | (target_index == 0)
    row_blocks = source_index * BLK_DEV + jax.random.randint(subkeys[2], grid_shape, 0, BLK_DEV)
    col_blocks = target_index * BLK_DEV + jax.random.randint(subkeys[3], grid_shape, 0, BLK_DEV)
    listed = jnp.stack([jnp.where(active, row_blocks, -1), jnp.where(active, col_blocks, -1)], axis=-1)
    return listed.astype(jnp.int32)


def block_scale(own_key, extent, cuts, smallest, top_value):
    def one(dim, blocks):
        draws = jax.random.uniform(jax.random.fold_in(jax.random.fold_in(own_key, 6), dim), (blocks,), jnp.float32, smallest / len(cuts), top_value / len(cuts))
        return jnp.repeat(jnp.exp(draws), extent[dim] // blocks).reshape((-1,) + (1,) * (len(extent) - dim - 1))

    gain = one(*cuts[0])
    for cut in cuts[1:]:
        gain = gain * one(*cut)
    return gain


def setup_inputs(seed: int = 0) -> dict:
    key_list = jax.random.split(jax.random.key(seed), 7)
    return {
        "positions": jnp.clip(jax.random.uniform(key_list[0], (3, NBLK, P_SIZE), jnp.float32, -1.0, 1.0) * block_scale(key_list[0], (3, NBLK, P_SIZE), ((1, 128),), -0.4, 0.0), -1.0, 1.0),
        "facing": jnp.clip(jax.random.uniform(key_list[1], (2, NBLK, P_SIZE), jnp.float32, -3.140625, 3.140625), -3.140625, 3.140625),
        "area": jnp.clip(jnp.exp(math.log(0.03125) - 2.0794415 * jax.random.uniform(key_list[2], (NBLK, P_SIZE), jnp.float32) ** block_scale(key_list[2], (NBLK, P_SIZE), ((0, 128),), -0.2, 0.2)), 0.00390625, 0.03125),
        "emission": jnp.clip(jnp.exp(math.log(2.0) - 2.9957323 * jax.random.uniform(key_list[3], (NBLK, BANDS, P_SIZE), jnp.float32) ** block_scale(key_list[3], (NBLK, BANDS, P_SIZE), ((0, 128),), -0.2, 0.2)), 0.1, 2.0),
        "reflect": jnp.clip(0.2 + 0.7 * jax.random.uniform(key_list[4], (NBLK, BANDS, P_SIZE), jnp.float32) ** block_scale(key_list[4], (NBLK, BANDS, P_SIZE), ((0, 128),), -0.2, 0.2), 0.2, 0.9),
        "pair_list": draw_pair_list(jax.random.fold_in(key_list[6], 71), 0),
    }


soften = 0.1


def unit_normals(facing):
    azimuth = facing[0]
    elevation = facing[1]
    return jnp.stack([jnp.cos(azimuth) * jnp.cos(elevation), jnp.sin(azimuth) * jnp.cos(elevation), jnp.sin(elevation)], axis=0)


def pack_geometry(positions, facing):
    normals = unit_normals(facing)
    return jnp.transpose(jnp.concatenate([positions, normals], axis=0), (1, 0, 2))


def coupling(row_geom, col_geom):
    offsets = [col_geom[:, axis_id, None, :] - row_geom[:, axis_id, :, None] for axis_id in range(3)]
    spread = offsets[0] * offsets[0] + offsets[1] * offsets[1] + offsets[2] * offsets[2] + soften
    nearside = row_geom[:, 3, :, None] * offsets[0] + row_geom[:, 4, :, None] * offsets[1] + row_geom[:, 5, :, None] * offsets[2]
    farside = col_geom[:, 3, None, :] * offsets[0] + col_geom[:, 4, None, :] * offsets[1] + col_geom[:, 5, None, :] * offsets[2]
    coupled = jnp.maximum(nearside, 0.0) * jnp.maximum(-farside, 0.0) / (jnp.pi * spread * spread)
    return coupled.astype(jnp.bfloat16)


def reference(positions, facing, area, emission, reflect, pair_list):
    geometry = pack_geometry(positions, facing)
    flat_list = pair_list.reshape(-1, 2).astype(jnp.int32)
    per_scan = 64
    extra = (-flat_list.shape[0]) % per_scan
    flat_list = jnp.concatenate([flat_list, jnp.full((extra, 2), -1, jnp.int32)], axis=0)
    active = flat_list[:, 0] >= 0
    row_ids = jnp.where(active, flat_list[:, 0], 0).astype(jnp.int32).reshape(-1, per_scan)
    col_ids = jnp.where(active, flat_list[:, 1], 0).astype(jnp.int32).reshape(-1, per_scan)
    weight_mask = jnp.where(active, 1.0, 0.0).astype(jnp.float32).reshape(-1, per_scan)
    radiosity = emission
    for sweep_index in range(SWEEPS):
        weighted = (area[:, None, :] * radiosity).astype(jnp.bfloat16)

        def accumulate(gathered, pieces):
            rows_now, cols_now, mask_now = pieces
            kernel = coupling(geometry[rows_now], geometry[cols_now]).astype(jnp.float32)
            col_values = weighted[cols_now].astype(jnp.float32)
            row_values = weighted[rows_now].astype(jnp.float32)
            row_terms = jnp.einsum("gij,gbj->gbi", kernel, col_values, precision=lax.Precision.HIGHEST) * mask_now[:, None, None]
            col_terms = jnp.einsum("gij,gbi->gbj", kernel, row_values, precision=lax.Precision.HIGHEST) * mask_now[:, None, None]
            gathered = gathered.at[rows_now].add(row_terms).at[cols_now].add(col_terms)
            return gathered, None

        gathered, unused = lax.scan(accumulate, jnp.zeros(emission.shape, jnp.float32), (row_ids, col_ids, weight_mask))
        radiosity = emission + reflect * gathered
    return radiosity
```

```python
import functools
import math

import jax
import jax.numpy as jnp
from jax import lax
from jax.experimental import pallas as pl
from jax.experimental.pallas import tpu as pltpu
from jax.sharding import PartitionSpec as P

MESH = pl.DeviceIdType.MESH
VMEM = pl.BlockSpec(memory_space=pltpu.VMEM)
SMEM = pl.BlockSpec(memory_space=pltpu.SMEM)
F32, BF16, I32 = jnp.float32, jnp.bfloat16, jnp.int32

NX, NY, NZ, NC = 4, 4, 16, 2
NS, NT = NX * NC, NZ
ROOT_PI = math.sqrt(math.pi)
SOFTEN = 0.1


def place():
    p = lax.axis_index("pairs")
    return p // (NZ * NC), lax.axis_index("rep"), (p // NC) % NZ, p % NC


def device(x, y, z, c):
    return {"pairs": (x * NZ + z) * NC + c, "rep": y}


def plane_peer(me, i):
    x, y, z, c = me
    return (x + i // (NY * NC)) % NX, (y + (i // NC) % NY) % NY, z, (c + i % NC) % NC


def line_peer(me, d):
    x, y, z, c = me
    return x, y, (z + d) % NZ, c


def greet(me):
    barrier = pltpu.get_barrier_semaphore()

    def plane(i, _):
        pl.semaphore_signal(barrier, inc=1, device_id=device(*plane_peer(me, i)), device_id_type=MESH)
        return 0

    def line(d, _):
        pl.semaphore_signal(barrier, inc=1, device_id=device(*line_peer(me, d)), device_id_type=MESH)
        return 0

    lax.fori_loop(1, NZ, line, 0)
    lax.fori_loop(1, NX * NY * NC, plane, 0)


def met():
    pl.semaphore_wait(pltpu.get_barrier_semaphore(), NX * NY * NC - 1 + NZ - 1)


def remote(src, dst, sems, i, peer):
    return pltpu.make_async_remote_copy(
        src_ref=src,
        dst_ref=dst,
        send_sem=sems.at[0, i],
        recv_sem=sems.at[1, i],
        device_id=device(*peer),
        device_id_type=MESH,
    )


def start_all(first, last, copy):
    def body(i, _):
        copy(i).start()
        return 0

    lax.fori_loop(first, last, body, 0)


def wait_all(first, last, copy):
    def body(i, _):
        copy(i).wait()
        return 0

    lax.fori_loop(first, last, body, 0)


def gather_kernel(pos_ref, facing_ref, area_ref, emission_ref, code_ref,
                  geo_s, geo_t, w_s, w_t, lists_ref,
                  own_geo, own_w, own_code, codes, sem_gt, sem_wt, sem_gs, sem_ws, sem_l):
    me = place()
    x, y, z, c = me
    mine = x * NC + c
    greet(me)
    azimuth, elevation = facing_ref[0], facing_ref[1]
    flat = jnp.cos(elevation)
    parts = [pos_ref[0], pos_ref[1], pos_ref[2],
             jnp.cos(azimuth) * flat, jnp.sin(azimuth) * flat, jnp.sin(elevation)]
    for k in range(4):
        for comp in range(6):
            own_geo[k, comp * 4 : comp * 4 + 4, :] = parts[comp][4 * k : 4 * k + 4, :]
        own_w[k] = jnp.concatenate(
            [area_ref[4 * k + b : 4 * k + b + 1, :] * emission_ref[4 * k + b] for b in range(4)], axis=0
        ).astype(BF16)
    own_code[...] = code_ref[...]
    met()

    def geo_line(d):
        return remote(own_geo.at[y], geo_t.at[z], sem_gt, d, line_peer(me, d))

    def w_line(d):
        return remote(own_w.at[y], w_t.at[z], sem_wt, d, line_peer(me, d))

    def near_peer(i):
        return (x + i // NC) % NX, y, z, (c + i % NC) % NC

    def geo_plane(i):
        return remote(own_geo, geo_s.at[pl.ds(4 * mine, 4)], sem_gs, i, near_peer(i))

    def w_plane(i):
        return remote(own_w, w_s.at[pl.ds(4 * mine, 4)], sem_ws, i, near_peer(i))

    def list_plane(i):
        return remote(own_code, codes.at[mine * NY + y], sem_l, i, plane_peer(me, i))

    start_all(1, NZ, geo_line)
    start_all(1, NZ, w_line)
    start_all(1, NX * NY * NC, list_plane)
    start_all(1, NS, geo_plane)
    start_all(1, NS, w_plane)
    geo_t[z] = own_geo[y]
    w_t[z] = own_w[y]
    geo_s[pl.ds(4 * mine, 4)] = own_geo[...]
    w_s[pl.ds(4 * mine, 4)] = own_w[...]
    codes[mine * NY + y] = own_code[...]
    wait_all(1, NX * NY * NC, list_plane)
    for s in range(NX * NY * NC):
        lists_ref[s : s + 1, :] = codes[s, 0:1, :]
    wait_all(1, NS, geo_plane)
    wait_all(1, NS, w_plane)
    wait_all(1, NZ, geo_line)
    wait_all(1, NZ, w_line)


def three(v):
    high = v.astype(BF16)
    rest = v - high.astype(F32)
    middle = rest.astype(BF16)
    return high, middle, (rest - middle.astype(F32)).astype(BF16)


def pair_kernel(lists_ref, geo_s, geo_t, w_s, w_t, acc_s, acc_t,
                g_s, g_t, v_s, v_t, spread_geo, order):
    x, y, z, c = place()
    acc_s[...] = jnp.zeros_like(acc_s)
    acc_t[...] = jnp.zeros_like(acc_t)

    def unpack(geo, w, g, v):
        def body(q, _):
            data = geo[q]
            normal = data[12:24]
            product = data[0:12] * normal
            square = data[0:12] * data[0:12]
            product = product[0:4] + product[4:8] + product[8:12]
            square = square[0:4] + square[4:8] + square[8:12]
            for half in range(2):
                lanes = slice(128 * half, 128 * half + 128)
                spread_geo[half, 0:24, :] = data[:, lanes]
                spread_geo[half, 24:28, :] = product[:, lanes]
                spread_geo[half, 28:32, :] = square[:, lanes]
                for b in range(4):
                    g[4 * q + b, :, lanes] = spread_geo[half, pl.ds(b, 8, stride=4), :]
            values = w[q].astype(F32)
            for b in range(4):
                v[4 * q + b] = values[8 * b : 8 * b + 8]
            return 0

        lax.fori_loop(0, geo.shape[0], body, 0)
        g[4 * geo.shape[0]] = jnp.zeros((8, 256), F32)
        v[4 * geo.shape[0]] = jnp.zeros((8, 256), F32)

    unpack(geo_s, w_s, g_s, v_s)
    unpack(geo_t, w_t, g_t, v_t)

    def scan_list(s, count):
        for zz in range(NZ):
            code = lists_ref[s, x * (NZ * NC) + zz * NC + c]
            keep = (code >= 0) & (((code >> 2) & 3) == y)
            order[count] = ((s >> 2) * 16 + (code >> 4)) | ((zz * 4 + (code & 3)) << 8)
            count = count + keep.astype(I32)
        return count

    count = lax.fori_loop(0, NX * NY * NC, scan_list, jnp.int32(0))
    order[count] = jnp.int32((4 * NS * 4) | ((4 * NT) << 8))

    row = lax.broadcasted_iota(I32, (8, 256), 0)
    unit = jnp.where(row == 0, 1.0, 0.0).astype(F32)
    zero = jnp.zeros((8, 256), F32)

    def one(slot):
        entry = order[slot]
        i, j = entry & 255, entry >> 8
        gi, gj = g_s[i], g_t[j]
        h, m, l = three(jnp.concatenate([gi, unit], axis=0))
        left = jnp.concatenate([h, h, m, h, l, m], axis=0).T
        near = jnp.where((row >= 3) & (row < 6), pltpu.roll(gj, 3, 0), jnp.where(row == 6, -1.0, 0.0))
        far = jnp.where(row < 3, pltpu.roll(gj, 5, 0), 0.0)
        far_low = jnp.where(row == 0, -pltpu.roll(gj, 2, 0), 0.0)
        dist = jnp.where(row < 3, (-2.0 * ROOT_PI) * gj, jnp.where(row == 7, ROOT_PI, 0.0))
        dist_low = jnp.where(row == 0, ROOT_PI * (pltpu.roll(gj, 1, 0) + SOFTEN), 0.0)
        right = jnp.concatenate(
            [
                jnp.concatenate([near, zero], axis=0),
                jnp.concatenate([far, far_low], axis=0),
                jnp.concatenate([dist, dist_low], axis=0),
            ],
            axis=1,
        )
        h, m, l = three(right)
        right = jnp.concatenate([h, m, h, l, h, m], axis=0)
        pieces = []
        for r in range(4):
            out = jnp.dot(left[64 * r : 64 * r + 64], right, preferred_element_type=F32)
            top = jnp.maximum(out[:, 0:256], 0.0) * jnp.maximum(out[:, 256:512], 0.0)
            inverse = pl.reciprocal(out[:, 512:768], approx=False)
            pieces.append((top * (inverse * inverse)).astype(BF16))
        kernel = jnp.concatenate(pieces, axis=0)
        row_terms = lax.dot_general(
            v_t[j].astype(BF16), kernel, (((1,), (1,)), ((), ())), preferred_element_type=F32
        )
        col_terms = jnp.dot(v_s[i].astype(BF16), kernel, preferred_element_type=F32)
        acc_s[i & 127] += row_terms
        acc_t[j & 63] += col_terms

    def two(turn, _):
        one(2 * turn)
        one(2 * turn + 1)
        return 0

    lax.fori_loop(0, (count + 1) // 2, two, 0)


def reduce_parts(me, acc_s, acc_t, got_s, got_t, sem_s, sem_t):
    x, y, z, c = me

    def line(d):
        peer = line_peer(me, d)
        return remote(acc_t.at[peer[2]], got_t.at[d], sem_t, d, peer)

    def plane(i):
        peer = plane_peer(me, i)
        return remote(acc_s.at[(peer[0] * NC + peer[3]) * 4 + peer[1]], got_s.at[i], sem_s, i, peer)

    start_all(1, NZ, line)
    start_all(1, NX * NY * NC, plane)
    wait_all(1, NX * NY * NC, plane)
    total = acc_s[(x * NC + c) * 4 + y] + acc_t[z]
    total = lax.fori_loop(1, NX * NY * NC, lambda i, t: t + got_s[i], total)
    wait_all(1, NZ, line)
    return lax.fori_loop(1, NZ, lambda d, t: t + got_t[d], total)


def turn_kernel(acc_s, acc_t, area_ref, emission_ref, reflect_ref, w_s, w_t,
                got_s, got_t, own_w, sem_s, sem_t, sem_ws, sem_wt):
    me = place()
    x, y, z, c = me
    greet(me)
    met()
    total = reduce_parts(me, acc_s, acc_t, got_s, got_t, sem_s, sem_t)
    radiosity = emission_ref[y] + reflect_ref[y] * total
    area = jnp.concatenate(
        [jnp.broadcast_to(area_ref[pl.ds(4 * y + b, 1), :], (8, 256)) for b in range(4)], axis=0
    )
    own_w[...] = (area * radiosity).astype(BF16)
    slot = (x * NC + c) * 4 + y

    def line(d):
        return remote(own_w, w_t.at[z], sem_wt, d, line_peer(me, d))

    def plane(i):
        return remote(own_w, w_s.at[slot], sem_ws, i, plane_peer(me, i))

    start_all(1, NZ, line)
    start_all(1, NX * NY * NC, plane)
    w_t[z] = own_w[...]
    w_s[slot] = own_w[...]
    wait_all(1, NX * NY * NC, plane)
    wait_all(1, NZ, line)


def last_kernel(acc_s, acc_t, emission_ref, reflect_ref, out_ref,
                got_s, got_t, own, sem_s, sem_t, sem_o):
    me = place()
    x, y, z, c = me
    greet(me)
    met()
    total = reduce_parts(me, acc_s, acc_t, got_s, got_t, sem_s, sem_t)
    own[...] = emission_ref[y] + reflect_ref[y] * total

    def across(i):
        return remote(own, out_ref.at[y], sem_o, i, (x, (y + i) % NY, z, c))

    start_all(1, NY, across)
    out_ref[y] = own[...]
    wait_all(1, NY, across)


def sems(n):
    return pltpu.SemaphoreType.DMA((2, n))


def shape(dims, dtype=F32):
    return jax.ShapeDtypeStruct(dims, dtype)


def call(kernel, ident, inputs, outputs, scratch, name, specs=None):
    params = {"vmem_limit_bytes": 60 * 1024 * 1024}
    if ident is not None:
        params.update(collective_id=ident, has_side_effects=True)
    return pl.pallas_call(
        kernel,
        out_shape=outputs,
        in_specs=specs or [VMEM] * len(inputs),
        out_specs=[VMEM] * len(outputs),
        scratch_shapes=scratch,
        compiler_params=pltpu.CompilerParams(**params),
        name=name,
    )(*inputs)


def pairs_call(lists, geo_s, geo_t, w_s, w_t):
    acc_s, acc_t = call(
        pair_kernel, None, (lists, geo_s, geo_t, w_s, w_t),
        [shape((16 * NS, 8, 256)), shape((4 * NT, 8, 256))],
        [pltpu.VMEM((16 * NS + 1, 8, 256), F32), pltpu.VMEM((4 * NT + 1, 8, 256), F32),
         pltpu.VMEM((16 * NS + 1, 8, 256), F32), pltpu.VMEM((4 * NT + 1, 8, 256), F32),
         pltpu.VMEM((2, 32, 128), F32), pltpu.SMEM((520,), I32)],
        "pairs", [SMEM] + [VMEM] * 4,
    )
    return acc_s.reshape(4 * NS, 32, 256), acc_t.reshape(NT, 32, 256)


def shards(positions, facing, area, emission, reflect, pair_list):
    held = pair_list.reshape(128, 2)
    code = jnp.where(held[:, 0] >= 0, (held[:, 0] % 16) * 16 + held[:, 1] % 16, -1)
    code = jnp.broadcast_to(code[None, :], (8, 128))
    plane = NX * NY * NC
    geo_s, geo_t, w_s, w_t, lists = call(
        gather_kernel, 0, (positions, facing, area, emission, code),
        [shape((4 * NS, 24, 256)), shape((NT, 24, 256)), shape((4 * NS, 32, 256), BF16),
         shape((NT, 32, 256), BF16), shape((plane, 128), I32)],
        [pltpu.VMEM((4, 24, 256), F32), pltpu.VMEM((4, 32, 256), BF16), pltpu.VMEM((8, 128), I32),
         pltpu.VMEM((plane, 8, 128), I32), sems(NZ), sems(NZ), sems(NS), sems(NS), sems(plane)],
        "gather",
    )

    emission4, reflect4 = emission.reshape(4, 32, 256), reflect.reshape(4, 32, 256)
    landing = [pltpu.VMEM((plane, 32, 256), F32), pltpu.VMEM((NZ, 32, 256), F32)]
    acc_s, acc_t = pairs_call(lists, geo_s, geo_t, w_s, w_t)
    w_s, w_t = call(
        turn_kernel, 1, (acc_s, acc_t, area, emission4, reflect4),
        [shape((4 * NS, 32, 256), BF16), shape((NT, 32, 256), BF16)],
        landing + [pltpu.VMEM((32, 256), BF16), sems(plane), sems(NZ), sems(plane), sems(NZ)],
        "turn",
    )
    acc_s, acc_t = pairs_call(lists, geo_s, geo_t, w_s, w_t)
    (out,) = call(
        last_kernel, 2, (acc_s, acc_t, emission4, reflect4), [shape((4, 32, 256))],
        landing + [pltpu.VMEM((32, 256), F32), sems(plane), sems(NZ), sems(NY)],
        "last",
    )
    return out.reshape(16, 8, 256)


def solution(mesh):
    placed = (
        P(None, "pairs", None),
        P(None, "pairs", None),
        P("pairs", None),
        P("pairs", None, None),
        P("pairs", None, None),
        P("pairs", "rep", None, None, None),
    )
    return jax.shard_map(
        shards, mesh=mesh, in_specs=placed, out_specs=P("pairs", None, None), check_vma=False
    )
```

```python
import functools
import math

import jax
import jax.numpy as jnp
from jax import lax
from jax.experimental import pallas as pl
from jax.experimental.pallas import tpu as pltpu
from jax.sharding import PartitionSpec as P

MESH = pl.DeviceIdType.MESH
VMEM = pl.BlockSpec(memory_space=pltpu.VMEM)
SMEM = pl.BlockSpec(memory_space=pltpu.SMEM)
F32, BF16, I32 = jnp.float32, jnp.bfloat16, jnp.int32

NX, NY, NZ, NC = 4, 4, 16, 2
NS, NT = NX * NC, NZ
ROOT_PI = math.sqrt(math.pi)
SOFTEN = 0.1


def place():
    p = lax.axis_index("pairs")
    return p // (NZ * NC), lax.axis_index("rep"), (p // NC) % NZ, p % NC


def device(x, y, z, c):
    return {"pairs": (x * NZ + z) * NC + c, "rep": y}


def plane_peer(me, i):
    x, y, z, c = me
    return (x + i // (NY * NC)) % NX, (y + (i // NC) % NY) % NY, z, (c + i % NC) % NC


def line_peer(me, d):
    x, y, z, c = me
    return x, y, (z + d) % NZ, c


def greet(me):
    barrier = pltpu.get_barrier_semaphore()

    def plane(i, _):
        pl.semaphore_signal(barrier, inc=1, device_id=device(*plane_peer(me, i)), device_id_type=MESH)
        return 0

    def line(d, _):
        pl.semaphore_signal(barrier, inc=1, device_id=device(*line_peer(me, d)), device_id_type=MESH)
        return 0

    lax.fori_loop(1, NZ, line, 0)
    lax.fori_loop(1, NX * NY * NC, plane, 0)


def met():
    pl.semaphore_wait(pltpu.get_barrier_semaphore(), NX * NY * NC - 1 + NZ - 1)


def remote(src, dst, sems, i, peer):
    return pltpu.make_async_remote_copy(
        src_ref=src,
        dst_ref=dst,
        send_sem=sems.at[0, i],
        recv_sem=sems.at[1, i],
        device_id=device(*peer),
        device_id_type=MESH,
    )


def start_all(first, last, copy):
    def body(i, _):
        copy(i).start()
        return 0

    lax.fori_loop(first, last, body, 0)


def wait_all(first, last, copy):
    def body(i, _):
        copy(i).wait()
        return 0

    lax.fori_loop(first, last, body, 0)


def gather_kernel(pos_ref, facing_ref, area_ref, emission_ref, code_ref,
                  geo_s, geo_t, w_s, w_t, lists_ref,
                  own_geo, own_w, own_code, codes, sem_gt, sem_wt, sem_gs, sem_ws, sem_l):
    me = place()
    x, y, z, c = me
    mine = x * NC + c
    greet(me)
    azimuth, elevation = facing_ref[0], facing_ref[1]
    flat = jnp.cos(elevation)
    parts = [pos_ref[0], pos_ref[1], pos_ref[2],
             jnp.cos(azimuth) * flat, jnp.sin(azimuth) * flat, jnp.sin(elevation)]
    for k in range(4):
        for comp in range(6):
            own_geo[k, comp * 4 : comp * 4 + 4, :] = parts[comp][4 * k : 4 * k + 4, :]
        own_w[k] = jnp.concatenate(
            [area_ref[4 * k + b : 4 * k + b + 1, :] * emission_ref[4 * k + b] for b in range(4)], axis=0
        ).astype(BF16)
    own_code[...] = code_ref[...]
    met()

    def geo_line(d):
        return remote(own_geo.at[y], geo_t.at[z], sem_gt, d, line_peer(me, d))

    def w_line(d):
        return remote(own_w.at[y], w_t.at[z], sem_wt, d, line_peer(me, d))

    def near_peer(i):
        return (x + i // NC) % NX, y, z, (c + i % NC) % NC

    def geo_plane(i):
        return remote(own_geo, geo_s.at[pl.ds(4 * mine, 4)], sem_gs, i, near_peer(i))

    def w_plane(i):
        return remote(own_w, w_s.at[pl.ds(4 * mine, 4)], sem_ws, i, near_peer(i))

    def list_plane(i):
        return remote(own_code, codes.at[mine * NY + y], sem_l, i, plane_peer(me, i))

    start_all(1, NZ, geo_line)
    start_all(1, NZ, w_line)
    start_all(1, NX * NY * NC, list_plane)
    start_all(1, NS, geo_plane)
    start_all(1, NS, w_plane)
    geo_t[z] = own_geo[y]
    w_t[z] = own_w[y]
    geo_s[pl.ds(4 * mine, 4)] = own_geo[...]
    w_s[pl.ds(4 * mine, 4)] = own_w[...]
    codes[mine * NY + y] = own_code[...]
    wait_all(1, NX * NY * NC, list_plane)
    for s in range(NX * NY * NC):
        lists_ref[s : s + 1, :] = codes[s, 0:1, :]
    code = lists_ref[...]
    lane = lax.broadcasted_iota(I32, code.shape, 1)
    owner = lax.broadcasted_iota(I32, code.shape, 0) >> 2
    ours = (code >= 0) & ((lane >> 5) == x) & ((lane & 1) == c) & (((code >> 2) & 3) == y)
    entry = (owner * 16 + (code >> 4)) | (((((lane & 31) >> 1) * 4) + (code & 3)) << 8)
    lists_ref[...] = jnp.where(ours, entry, -1)
    wait_all(1, NS, geo_plane)
    wait_all(1, NS, w_plane)
    wait_all(1, NZ, geo_line)
    wait_all(1, NZ, w_line)


def three(v):
    high = v.astype(BF16)
    rest = v - high.astype(F32)
    middle = rest.astype(BF16)
    return high, middle, (rest - middle.astype(F32)).astype(BF16)


PAIRS_KEPT = 128
RING = 4
UNUSED = (16 * NS) | ((4 * NT) << 8)


def unpack_geometry(q, geo, g, spread_geo):
    data = geo[q]
    product = data[0:12] * data[12:24]
    square = data[0:12] * data[0:12]
    product = product[0:4] + product[4:8] + product[8:12]
    square = square[0:4] + square[4:8] + square[8:12]
    for half in range(2):
        lanes = slice(128 * half, 128 * half + 128)
        spread_geo[half, 0:24, :] = data[:, lanes]
        spread_geo[half, 24:28, :] = product[:, lanes]
        spread_geo[half, 28:32, :] = square[:, lanes]
        for b in range(4):
            g[4 * q + b, :, lanes] = spread_geo[half, pl.ds(b, 8, stride=4), :]


def unpack_values(q, w, v):
    values = w[q].astype(F32)
    for b in range(4):
        v[4 * q + b] = values[8 * b : 8 * b + 8]


def clear_tail(*refs):
    for ref in refs:
        ref[ref.shape[0] - 1] = jnp.zeros((8, 256), F32)


def couple(entry, g_s, g_t):
    gi, gj = g_s[entry & 255], g_t[entry >> 8]
    row = lax.broadcasted_iota(I32, (8, 256), 0)
    unit = jnp.where(row == 0, 1.0, 0.0).astype(F32)
    zero = jnp.zeros((8, 256), F32)
    h, m, l = three(jnp.concatenate([gi, unit], axis=0))
    left = jnp.concatenate([h, h, m, h, l, m], axis=0).T
    near = jnp.where((row >= 3) & (row < 6), pltpu.roll(gj, 3, 0), jnp.where(row == 6, -1.0, 0.0))
    far = jnp.where(row < 3, pltpu.roll(gj, 5, 0), 0.0)
    far_low = jnp.where(row == 0, -pltpu.roll(gj, 2, 0), 0.0)
    dist = jnp.where(row < 3, (-2.0 * ROOT_PI) * gj, jnp.where(row == 7, ROOT_PI, 0.0))
    dist_low = jnp.where(row == 0, ROOT_PI * (pltpu.roll(gj, 1, 0) + SOFTEN), 0.0)
    outs = []
    for top, low in ((near, zero), (far, far_low), (dist, dist_low)):
        h, m, l = three(jnp.concatenate([top, low], axis=0))
        right = jnp.concatenate([h, m, h, l, h, m], axis=0)
        outs.append(jnp.dot(left, right, preferred_element_type=F32))
    near, far, dist = outs
    inverse = pl.reciprocal(dist, approx=False)
    return (jnp.maximum(near, 0.0) * jnp.maximum(far, 0.0) * (inverse * inverse)).astype(BF16)


def apply(entry, kernel, v_s, v_t, acc_s, acc_t):
    i, j = entry & 255, entry >> 8
    acc_s[i & (16 * NS - 1)] += lax.dot_general(
        v_t[j].astype(BF16), kernel, (((1,), (1,)), ((), ())), preferred_element_type=F32
    )
    acc_t[j & (4 * NT - 1)] += jnp.dot(v_s[i].astype(BF16), kernel, preferred_element_type=F32)


def pair_kernel(lists_ref, geo_s, geo_t, w_s, w_t, acc_s, acc_t, order, cache,
                g_s, g_t, v_s, v_t, spread_geo, held, sem):
    x, y, z, c = place()
    acc_s[...] = jnp.zeros_like(acc_s)
    acc_t[...] = jnp.zeros_like(acc_t)
    held[...] = jnp.zeros_like(held)
    clear_tail(g_s, g_t, v_s, v_t)
    base = x * (NZ * NC) + c

    def prepare_t(q, _):
        unpack_geometry(q, geo_t, g_t, spread_geo)
        unpack_values(q, w_t, v_t)
        return 0

    def prepare_s(q, count):
        unpack_geometry(q, geo_s, g_s, spread_geo)
        unpack_values(q, w_s, v_s)
        for zz in range(NZ):
            entry = lists_ref[q, base + zz * NC]
            order[count] = entry
            count = count + 1 + (entry >> 31)
        return count

    lax.fori_loop(0, NT, prepare_t, 0)
    count = lax.fori_loop(0, 4 * NS, prepare_s, jnp.int32(1))
    order[count] = jnp.int32(UNUSED)
    order[0] = count - 1
    turns = count >> 1

    def keep(u):
        return pltpu.make_async_copy(held.at[u & (RING - 1)], cache.at[u], sem.at[u & (RING - 1)])

    def turn(t, last):
        @pl.when((t >= 1) & (t <= PAIRS_KEPT))
        def _():
            keep(t - 1).start()

        @pl.when((t >= RING) & (t < PAIRS_KEPT + RING))
        def _():
            keep(t - RING).wait()

        now = (order[2 * t + 1], order[2 * t + 2])
        for k in range(2):
            apply(last[k], held[(t + RING - 1) & (RING - 1), k], v_s, v_t, acc_s, acc_t)
        for k in range(2):
            held[t & (RING - 1), k] = couple(now[k], g_s, g_t)
        return now

    nothing = (jnp.int32(UNUSED), jnp.int32(UNUSED))
    last = lax.fori_loop(0, turns, turn, nothing)

    @pl.when((turns >= 1) & (turns <= PAIRS_KEPT))
    def _():
        keep(turns - 1).start()

    for k in range(2):
        apply(last[k], held[(turns + RING - 1) & (RING - 1), k], v_s, v_t, acc_s, acc_t)

    def drain(u, _):
        keep(u).wait()
        return 0

    lax.fori_loop(jnp.maximum(turns - RING, 0), jnp.minimum(turns, PAIRS_KEPT), drain, 0)


DEPTH = 8


def again_kernel(order, geo_s, geo_t, w_s, w_t, cache, acc_s, acc_t,
                 g_s, g_t, v_s, v_t, spread_geo, held, sem):
    turns = (order[0] + 1) >> 1
    kept = jnp.minimum(turns, PAIRS_KEPT)

    def fetch(u):
        return pltpu.make_async_copy(cache.at[u], held.at[u & (DEPTH - 1)], sem.at[u & (DEPTH - 1)])

    def begin(u, _):
        fetch(u).start()
        return 0

    lax.fori_loop(0, jnp.minimum(kept, DEPTH), begin, 0)
    acc_s[...] = jnp.zeros_like(acc_s)
    acc_t[...] = jnp.zeros_like(acc_t)
    clear_tail(g_s, g_t, v_s, v_t)

    def prepare_s(q, _):
        unpack_values(q, w_s, v_s)
        return 0

    def prepare_t(q, _):
        unpack_values(q, w_t, v_t)
        return 0

    lax.fori_loop(0, 4 * NS, prepare_s, 0)
    lax.fori_loop(0, NT, prepare_t, 0)

    def turn(t, _):
        fetch(t).wait()
        for k in range(2):
            apply(order[2 * t + 1 + k], held[t & (DEPTH - 1), k], v_s, v_t, acc_s, acc_t)

        @pl.when(t + DEPTH < kept)
        def _():
            fetch(t + DEPTH).start()

        return 0

    lax.fori_loop(0, kept, turn, 0)

    @pl.when(turns > PAIRS_KEPT)
    def _():
        def shape_s(q, _):
            unpack_geometry(q, geo_s, g_s, spread_geo)
            return 0

        def shape_t(q, _):
            unpack_geometry(q, geo_t, g_t, spread_geo)
            return 0

        def more(t, _):
            entry = order[t]
            apply(entry, couple(entry, g_s, g_t), v_s, v_t, acc_s, acc_t)
            return 0

        lax.fori_loop(0, 4 * NS, shape_s, 0)
        lax.fori_loop(0, NT, shape_t, 0)
        lax.fori_loop(2 * PAIRS_KEPT + 1, 2 * turns + 1, more, 0)


def reduce_parts(me, acc_s, acc_t, got_s, got_t, sem_s, sem_t):
    x, y, z, c = me

    def line(d):
        peer = line_peer(me, d)
        return remote(acc_t.at[peer[2]], got_t.at[d], sem_t, d, peer)

    def plane(i):
        peer = plane_peer(me, i)
        return remote(acc_s.at[(peer[0] * NC + peer[3]) * 4 + peer[1]], got_s.at[i], sem_s, i, peer)

    start_all(1, NZ, line)
    start_all(1, NX * NY * NC, plane)
    wait_all(1, NX * NY * NC, plane)
    total = acc_s[(x * NC + c) * 4 + y] + acc_t[z]
    total = lax.fori_loop(1, NX * NY * NC, lambda i, t: t + got_s[i], total)
    wait_all(1, NZ, line)
    return lax.fori_loop(1, NZ, lambda d, t: t + got_t[d], total)


def turn_kernel(acc_s, acc_t, area_ref, emission_ref, reflect_ref, w_s, w_t,
                got_s, got_t, own_w, sem_s, sem_t, sem_ws, sem_wt):
    me = place()
    x, y, z, c = me
    greet(me)
    met()
    total = reduce_parts(me, acc_s, acc_t, got_s, got_t, sem_s, sem_t)
    radiosity = emission_ref[y] + reflect_ref[y] * total
    area = jnp.concatenate(
        [jnp.broadcast_to(area_ref[pl.ds(4 * y + b, 1), :], (8, 256)) for b in range(4)], axis=0
    )
    own_w[...] = (area * radiosity).astype(BF16)
    slot = (x * NC + c) * 4 + y

    def line(d):
        return remote(own_w, w_t.at[z], sem_wt, d, line_peer(me, d))

    def plane(i):
        return remote(own_w, w_s.at[slot], sem_ws, i, plane_peer(me, i))

    start_all(1, NZ, line)
    start_all(1, NX * NY * NC, plane)
    w_t[z] = own_w[...]
    w_s[slot] = own_w[...]
    wait_all(1, NX * NY * NC, plane)
    wait_all(1, NZ, line)


def last_kernel(acc_s, acc_t, emission_ref, reflect_ref, out_ref,
                got_s, got_t, own, sem_s, sem_t, sem_o):
    me = place()
    x, y, z, c = me
    greet(me)
    met()
    total = reduce_parts(me, acc_s, acc_t, got_s, got_t, sem_s, sem_t)
    own[...] = emission_ref[y] + reflect_ref[y] * total

    def across(i):
        return remote(own, out_ref.at[y], sem_o, i, (x, (y + i) % NY, z, c))

    start_all(1, NY, across)
    out_ref[y] = own[...]
    wait_all(1, NY, across)


def sems(n):
    return pltpu.SemaphoreType.DMA((2, n))


def shape(dims, dtype=F32):
    return jax.ShapeDtypeStruct(dims, dtype)


def call(kernel, ident, inputs, outputs, scratch, name, specs=None, out_specs=None):
    params = {"vmem_limit_bytes": 60 * 1024 * 1024}
    if ident is not None:
        params.update(collective_id=ident, has_side_effects=True)
    return pl.pallas_call(
        kernel,
        out_shape=outputs,
        in_specs=specs or [VMEM] * len(inputs),
        out_specs=out_specs or [VMEM] * len(outputs),
        scratch_shapes=scratch,
        compiler_params=pltpu.CompilerParams(**params),
        name=name,
    )(*inputs)


ANY = pl.BlockSpec(memory_space=pl.ANY)


def pairs_call(first, lists, geo_s, geo_t, w_s, w_t, cache=None):
    outputs = [shape((16 * NS, 8, 256)), shape((4 * NT, 8, 256))]
    scratch = [pltpu.VMEM((16 * NS + 1, 8, 256), F32), pltpu.VMEM((4 * NT + 1, 8, 256), F32),
               pltpu.VMEM((16 * NS + 1, 8, 256), F32), pltpu.VMEM((4 * NT + 1, 8, 256), F32),
               pltpu.VMEM((2, 32, 128), F32)]
    depth = RING if first else DEPTH
    scratch += [pltpu.VMEM((depth, 2, 256, 256), BF16), pltpu.SemaphoreType.DMA((depth,))]
    if first:
        outputs += [shape((544,), I32), shape((PAIRS_KEPT, 2, 256, 256), BF16)]
        acc_s, acc_t, order, cache = call(
            pair_kernel, None, (lists, geo_s, geo_t, w_s, w_t), outputs, scratch, "pairs",
            [SMEM] + [VMEM] * 4, [VMEM, VMEM, SMEM, ANY],
        )
    else:
        acc_s, acc_t = call(
            again_kernel, None, (lists, geo_s, geo_t, w_s, w_t, cache), outputs, scratch, "again",
            [SMEM] + [VMEM] * 4 + [ANY],
        )
        order = lists
    return acc_s.reshape(4 * NS, 32, 256), acc_t.reshape(NT, 32, 256), order, cache


def shards(positions, facing, area, emission, reflect, pair_list):
    held = pair_list.reshape(128, 2)
    code = jnp.where(held[:, 0] >= 0, (held[:, 0] % 16) * 16 + held[:, 1] % 16, -1)
    code = jnp.broadcast_to(code[None, :], (8, 128))
    plane = NX * NY * NC
    geo_s, geo_t, w_s, w_t, lists = call(
        gather_kernel, 0, (positions, facing, area, emission, code),
        [shape((4 * NS, 24, 256)), shape((NT, 24, 256)), shape((4 * NS, 32, 256), BF16),
         shape((NT, 32, 256), BF16), shape((plane, 128), I32)],
        [pltpu.VMEM((4, 24, 256), F32), pltpu.VMEM((4, 32, 256), BF16), pltpu.VMEM((8, 128), I32),
         pltpu.VMEM((plane, 8, 128), I32), sems(NZ), sems(NZ), sems(NS), sems(NS), sems(plane)],
        "gather",
    )

    emission4, reflect4 = emission.reshape(4, 32, 256), reflect.reshape(4, 32, 256)
    landing = [pltpu.VMEM((plane, 32, 256), F32), pltpu.VMEM((NZ, 32, 256), F32)]
    acc_s, acc_t, order, cache = pairs_call(True, lists, geo_s, geo_t, w_s, w_t)
    w_s, w_t = call(
        turn_kernel, 1, (acc_s, acc_t, area, emission4, reflect4),
        [shape((4 * NS, 32, 256), BF16), shape((NT, 32, 256), BF16)],
        landing + [pltpu.VMEM((32, 256), BF16), sems(plane), sems(NZ), sems(plane), sems(NZ)],
        "turn",
    )
    acc_s, acc_t, _, _ = pairs_call(False, order, geo_s, geo_t, w_s, w_t, cache)
    (out,) = call(
        last_kernel, 2, (acc_s, acc_t, emission4, reflect4), [shape((4, 32, 256))],
        landing + [pltpu.VMEM((32, 256), F32), sems(plane), sems(NZ), sems(NY)],
        "last",
    )
    return out.reshape(16, 8, 256)


def solution(mesh):
    placed = (
        P(None, "pairs", None),
        P(None, "pairs", None),
        P("pairs", None),
        P("pairs", None, None),
        P("pairs", None, None),
        P("pairs", "rep", None, None, None),
    )
    return jax.shard_map(
        shards, mesh=mesh, in_specs=placed, out_specs=P("pairs", None, None), check_vma=False
    )
```

```python
import functools
import math

import jax
import jax.numpy as jnp
from jax import lax
from jax.experimental import pallas as pl
from jax.experimental.pallas import tpu as pltpu
from jax.sharding import PartitionSpec as P

MESH = pl.DeviceIdType.MESH
VMEM = pl.BlockSpec(memory_space=pltpu.VMEM)
SMEM = pl.BlockSpec(memory_space=pltpu.SMEM)
F32, BF16, I32 = jnp.float32, jnp.bfloat16, jnp.int32

NX, NY, NZ, NC = 4, 4, 16, 2
NS, NT = NX * NC, NZ
ROOT_PI = math.sqrt(math.pi)
SOFTEN = 0.1


def place():
    p = lax.axis_index("pairs")
    return p // (NZ * NC), lax.axis_index("rep"), (p // NC) % NZ, p % NC


def device(x, y, z, c):
    return {"pairs": (x * NZ + z) * NC + c, "rep": y}


def plane_peer(me, i):
    x, y, z, c = me
    return (x + i // (NY * NC)) % NX, (y + (i // NC) % NY) % NY, z, (c + i % NC) % NC


def line_peer(me, d):
    x, y, z, c = me
    return x, y, (z + d + NZ) % NZ, c


FAR = (6, -6, 3, -3)
NEAR = (1, -1)
LINE = (1, -1, 2, -2, 3, -3, 6, -6)


def greet(me):
    barrier = pltpu.get_barrier_semaphore()
    for d in LINE:
        pl.semaphore_signal(barrier, inc=1, device_id=device(*line_peer(me, d)), device_id_type=MESH)

    def plane(i, _):
        pl.semaphore_signal(barrier, inc=1, device_id=device(*plane_peer(me, i)), device_id_type=MESH)
        return 0

    lax.fori_loop(1, NX * NY * NC, plane, 0)


def met():
    pl.semaphore_wait(pltpu.get_barrier_semaphore(), NX * NY * NC - 1 + len(LINE))


def remote(src, dst, sems, i, peer):
    return pltpu.make_async_remote_copy(
        src_ref=src,
        dst_ref=dst,
        send_sem=sems.at[0, i],
        recv_sem=sems.at[1, i],
        device_id=device(*peer),
        device_id_type=MESH,
    )


def start_all(first, last, copy):
    def body(i, _):
        copy(i).start()
        return 0

    lax.fori_loop(first, last, body, 0)


def wait_all(first, last, copy):
    def body(i, _):
        copy(i).wait()
        return 0

    lax.fori_loop(first, last, body, 0)


def line_gather(me, own, into, sems):
    z = me[2]
    first = [remote(own, into.at[z], sems, n, line_peer(me, h)) for n, h in enumerate(FAR + NEAR)]
    for copy in first:
        copy.start()

    def finish():
        copies = []
        for n, h in enumerate(FAR):
            first[n].wait_recv()
            source = (z - h + NZ) % NZ
            steps = NEAR + (-2,) if h == -6 else NEAR
            for k, e in enumerate(steps):
                copy = remote(into.at[source], into.at[source], sems, 6 + 3 * n + k, line_peer(me, e))
                copy.start()
                copies.append(copy)
        first[4].wait_recv()
        first[5].wait_recv()
        for copy in copies:
            copy.wait_recv()
        for copy in first + copies:
            copy.wait_send()

    return finish


LINE_GATHER = 18


def gather_kernel(pos_ref, facing_ref, area_ref, emission_ref, code_ref,
                  geo_s, geo_t, w_s, w_t, lists_ref,
                  own_geo, own_w, own_code, codes, sem_gt, sem_wt, sem_gs, sem_ws, sem_l):
    me = place()
    x, y, z, c = me
    mine = x * NC + c
    greet(me)
    azimuth, elevation = facing_ref[0], facing_ref[1]
    flat = jnp.cos(elevation)
    parts = [pos_ref[0], pos_ref[1], pos_ref[2],
             jnp.cos(azimuth) * flat, jnp.sin(azimuth) * flat, jnp.sin(elevation)]
    for k in range(4):
        for comp in range(6):
            own_geo[k, comp * 4 : comp * 4 + 4, :] = parts[comp][4 * k : 4 * k + 4, :]
        own_w[k] = jnp.concatenate(
            [area_ref[4 * k + b : 4 * k + b + 1, :] * emission_ref[4 * k + b] for b in range(4)], axis=0
        ).astype(BF16)
    own_code[...] = code_ref[...]
    met()

    def across(own, into, sems, dx):
        return remote(own, into.at[pl.ds(4 * mine, 4)], sems, dx, ((x + dx) % NX, y, z, c))

    def beside(own, into, sems, dx):
        there = pl.ds(4 * (((x - dx + NX) % NX) * NC + c), 4)
        source = own if dx == 0 else into.at[there]
        return remote(source, into.at[there], sems, NX + dx, (x, y, z, 1 - c))

    def list_plane(i):
        return remote(own_code, codes.at[mine * NY + y], sem_l, i, plane_peer(me, i))

    plane = ((own_geo, geo_s, sem_gs), (own_w, w_s, sem_ws))
    line = (line_gather(me, own_geo.at[y], geo_t, sem_gt), line_gather(me, own_w.at[y], w_t, sem_wt))
    crossing = [across(*args, dx) for args in plane for dx in range(1, NX)]
    siblings = [beside(*args, dx) for args in plane for dx in range(NX)]
    for copy in crossing + [siblings[0], siblings[NX]]:
        copy.start()
    start_all(1, NX * NY * NC, list_plane)
    geo_t[z] = own_geo[y]
    w_t[z] = own_w[y]
    geo_s[pl.ds(4 * mine, 4)] = own_geo[...]
    w_s[pl.ds(4 * mine, 4)] = own_w[...]
    codes[mine * NY + y] = own_code[...]
    for n in range(2):
        for dx in range(1, NX):
            crossing[n * (NX - 1) + dx - 1].wait_recv()
            siblings[n * NX + dx].start()
    wait_all(1, NX * NY * NC, list_plane)
    for s in range(NX * NY * NC):
        lists_ref[s : s + 1, :] = codes[s, 0:1, :]
    code = lists_ref[...]
    lane = lax.broadcasted_iota(I32, code.shape, 1)
    owner = lax.broadcasted_iota(I32, code.shape, 0) >> 2
    ours = (code >= 0) & ((lane >> 5) == x) & ((lane & 1) == c) & (((code >> 2) & 3) == y)
    entry = (owner * 16 + (code >> 4)) | (((((lane & 31) >> 1) * 4) + (code & 3)) << 8)
    lists_ref[...] = jnp.where(ours, entry, -1)
    for finish in line:
        finish()
    for copy in crossing:
        copy.wait_send()
    for copy in siblings:
        copy.wait()


def three(v):
    high = v.astype(BF16)
    rest = v - high.astype(F32)
    middle = rest.astype(BF16)
    return high, middle, (rest - middle.astype(F32)).astype(BF16)


PAIRS_KEPT = 128
RING = 4
UNUSED = (16 * NS) | ((4 * NT) << 8)


def unpack_geometry(q, geo, g, spread_geo):
    data = geo[q]
    product = data[0:12] * data[12:24]
    square = data[0:12] * data[0:12]
    product = product[0:4] + product[4:8] + product[8:12]
    square = square[0:4] + square[4:8] + square[8:12]
    for half in range(2):
        lanes = slice(128 * half, 128 * half + 128)
        spread_geo[half, 0:24, :] = data[:, lanes]
        spread_geo[half, 24:28, :] = product[:, lanes]
        spread_geo[half, 28:32, :] = square[:, lanes]
        for b in range(4):
            g[4 * q + b, :, lanes] = spread_geo[half, pl.ds(b, 8, stride=4), :]


def unpack_values(q, w, v):
    values = w[q].astype(F32)
    for b in range(4):
        v[4 * q + b] = values[8 * b : 8 * b + 8]


def clear_tail(*refs):
    for ref in refs:
        ref[ref.shape[0] - 1] = jnp.zeros((8, 256), F32)


def couple(entry, g_s, g_t):
    gi, gj = g_s[entry & 255], g_t[entry >> 8]
    row = lax.broadcasted_iota(I32, (8, 256), 0)
    unit = jnp.where(row == 0, 1.0, 0.0).astype(F32)
    zero = jnp.zeros((8, 256), F32)
    h, m, l = three(jnp.concatenate([gi, unit], axis=0))
    left = jnp.concatenate([h, h, m, h, l, m], axis=0).T
    near = jnp.where((row >= 3) & (row < 6), pltpu.roll(gj, 3, 0), jnp.where(row == 6, -1.0, 0.0))
    far = jnp.where(row < 3, pltpu.roll(gj, 5, 0), 0.0)
    far_low = jnp.where(row == 0, -pltpu.roll(gj, 2, 0), 0.0)
    dist = jnp.where(row < 3, (-2.0 * ROOT_PI) * gj, jnp.where(row == 7, ROOT_PI, 0.0))
    dist_low = jnp.where(row == 0, ROOT_PI * (pltpu.roll(gj, 1, 0) + SOFTEN), 0.0)
    outs = []
    for top, low in ((near, zero), (far, far_low), (dist, dist_low)):
        h, m, l = three(jnp.concatenate([top, low], axis=0))
        right = jnp.concatenate([h, m, h, l, h, m], axis=0)
        outs.append(jnp.dot(left, right, preferred_element_type=F32))
    near, far, dist = outs
    inverse = pl.reciprocal(dist, approx=False)
    return (jnp.maximum(near, 0.0) * jnp.maximum(far, 0.0) * (inverse * inverse)).astype(BF16)


def apply(entry, kernel, v_s, v_t, acc_s, acc_t):
    i, j = entry & 255, entry >> 8
    acc_s[i & (16 * NS - 1)] += lax.dot_general(
        v_t[j].astype(BF16), kernel, (((1,), (1,)), ((), ())), preferred_element_type=F32
    )
    acc_t[j & (4 * NT - 1)] += jnp.dot(v_s[i].astype(BF16), kernel, preferred_element_type=F32)


def pair_kernel(lists_ref, geo_s, geo_t, w_s, w_t, acc_s, acc_t, order, cache,
                g_s, g_t, v_s, v_t, spread_geo, held, sem):
    x, y, z, c = place()
    acc_s[...] = jnp.zeros_like(acc_s)
    acc_t[...] = jnp.zeros_like(acc_t)
    held[...] = jnp.zeros_like(held)
    clear_tail(g_s, g_t, v_s, v_t)
    base = x * (NZ * NC) + c

    def prepare_t(q, _):
        unpack_geometry(q, geo_t, g_t, spread_geo)
        unpack_values(q, w_t, v_t)
        return 0

    def prepare_s(q, count):
        unpack_geometry(q, geo_s, g_s, spread_geo)
        unpack_values(q, w_s, v_s)
        for zz in range(NZ):
            entry = lists_ref[q, base + zz * NC]
            order[count] = entry
            count = count + 1 + (entry >> 31)
        return count

    lax.fori_loop(0, NT, prepare_t, 0)
    count = lax.fori_loop(0, 4 * NS, prepare_s, jnp.int32(1))
    order[count] = jnp.int32(UNUSED)
    order[0] = count - 1
    turns = count >> 1

    def keep(u):
        return pltpu.make_async_copy(held.at[u & (RING - 1)], cache.at[u], sem.at[u & (RING - 1)])

    def turn(t, last):
        @pl.when((t >= 1) & (t <= PAIRS_KEPT))
        def _():
            keep(t - 1).start()

        @pl.when((t >= RING) & (t < PAIRS_KEPT + RING))
        def _():
            keep(t - RING).wait()

        now = (order[2 * t + 1], order[2 * t + 2])
        for k in range(2):
            apply(last[k], held[(t + RING - 1) & (RING - 1), k], v_s, v_t, acc_s, acc_t)
        for k in range(2):
            held[t & (RING - 1), k] = couple(now[k], g_s, g_t)
        return now

    nothing = (jnp.int32(UNUSED), jnp.int32(UNUSED))
    last = lax.fori_loop(0, turns, turn, nothing)

    @pl.when((turns >= 1) & (turns <= PAIRS_KEPT))
    def _():
        keep(turns - 1).start()

    for k in range(2):
        apply(last[k], held[(turns + RING - 1) & (RING - 1), k], v_s, v_t, acc_s, acc_t)

    def drain(u, _):
        keep(u).wait()
        return 0

    lax.fori_loop(jnp.maximum(turns - RING, 0), jnp.minimum(turns, PAIRS_KEPT), drain, 0)


DEPTH = 8


def again_kernel(order, geo_s, geo_t, w_s, w_t, cache, acc_s, acc_t,
                 g_s, g_t, v_s, v_t, spread_geo, held, sem):
    turns = (order[0] + 1) >> 1
    kept = jnp.minimum(turns, PAIRS_KEPT)

    def fetch(u):
        return pltpu.make_async_copy(cache.at[u], held.at[u & (DEPTH - 1)], sem.at[u & (DEPTH - 1)])

    def begin(u, _):
        fetch(u).start()
        return 0

    lax.fori_loop(0, jnp.minimum(kept, DEPTH), begin, 0)
    acc_s[...] = jnp.zeros_like(acc_s)
    acc_t[...] = jnp.zeros_like(acc_t)
    clear_tail(g_s, g_t, v_s, v_t)

    def prepare_s(q, _):
        unpack_values(q, w_s, v_s)
        return 0

    def prepare_t(q, _):
        unpack_values(q, w_t, v_t)
        return 0

    lax.fori_loop(0, 4 * NS, prepare_s, 0)
    lax.fori_loop(0, NT, prepare_t, 0)

    def turn(t, _):
        fetch(t).wait()
        for k in range(2):
            apply(order[2 * t + 1 + k], held[t & (DEPTH - 1), k], v_s, v_t, acc_s, acc_t)

        @pl.when(t + DEPTH < kept)
        def _():
            fetch(t + DEPTH).start()

        return 0

    lax.fori_loop(0, kept, turn, 0)

    @pl.when(turns > PAIRS_KEPT)
    def _():
        def shape_s(q, _):
            unpack_geometry(q, geo_s, g_s, spread_geo)
            return 0

        def shape_t(q, _):
            unpack_geometry(q, geo_t, g_t, spread_geo)
            return 0

        def more(t, _):
            entry = order[t]
            apply(entry, couple(entry, g_s, g_t), v_s, v_t, acc_s, acc_t)
            return 0

        lax.fori_loop(0, 4 * NS, shape_s, 0)
        lax.fori_loop(0, NT, shape_t, 0)
        lax.fori_loop(2 * PAIRS_KEPT + 1, 2 * turns + 1, more, 0)


def reduce_parts(me, acc_s, acc_t, got_s, got_t, sum_t, far_t, sem_s, sem_t):
    x, y, z, c = me

    def plane(i):
        peer = plane_peer(me, i)
        return remote(acc_s.at[(peer[0] * NC + peer[3]) * 4 + peer[1]], got_s.at[i], sem_s, i, peer)

    def toward(n, h, k, e):
        piece = acc_t.at[(z + e - h + NZ) % NZ]
        return remote(piece, got_t.at[3 * n + k], sem_t, 3 * n + k, line_peer(me, e))

    hubs = FAR + (0,)
    near = [[toward(n, h, k, e) for k, e in enumerate(NEAR + (2,) if h == -6 else NEAR)]
            for n, h in enumerate(hubs)]
    for copies in near:
        for copy in copies:
            copy.start()
    start_all(1, NX * NY * NC, plane)
    far = []
    for n, h in enumerate(hubs):
        part = acc_t[(z - h + NZ) % NZ]
        for k, copy in enumerate(near[n]):
            copy.wait_recv()
            part = part + got_t[3 * n + k]
        if h:
            sum_t[n] = part
            far.append(remote(sum_t.at[n], far_t.at[n], sem_t, 15 + n, line_peer(me, -h)))
            far[n].start()
    total = part + acc_s[(x * NC + c) * 4 + y]
    wait_all(1, NX * NY * NC, plane)
    total = lax.fori_loop(1, NX * NY * NC, lambda i, t: t + got_s[i], total)
    for n, copy in enumerate(far):
        copy.wait_recv()
        total = total + far_t[n]
    for copies in near:
        for copy in copies:
            copy.wait_send()
    for copy in far:
        copy.wait_send()
    return total


LINE_SUM = 19


def turn_kernel(acc_s, acc_t, area_ref, emission_ref, reflect_ref, w_s, w_t,
                got_s, got_t, sum_t, far_t, own_w, sem_s, sem_t, sem_ws, sem_wt):
    me = place()
    x, y, z, c = me
    greet(me)
    met()
    total = reduce_parts(me, acc_s, acc_t, got_s, got_t, sum_t, far_t, sem_s, sem_t)
    radiosity = emission_ref[y] + reflect_ref[y] * total
    area = jnp.concatenate(
        [jnp.broadcast_to(area_ref[pl.ds(4 * y + b, 1), :], (8, 256)) for b in range(4)], axis=0
    )
    own_w[...] = (area * radiosity).astype(BF16)
    slot = (x * NC + c) * 4 + y

    def plane(i):
        return remote(own_w, w_s.at[slot], sem_ws, i, plane_peer(me, i))

    finish = line_gather(me, own_w, w_t, sem_wt)
    start_all(1, NX * NY * NC, plane)
    w_t[z] = own_w[...]
    w_s[slot] = own_w[...]
    finish()
    wait_all(1, NX * NY * NC, plane)


def last_kernel(acc_s, acc_t, emission_ref, reflect_ref, out_ref,
                got_s, got_t, sum_t, far_t, own, sem_s, sem_t, sem_o):
    me = place()
    x, y, z, c = me
    greet(me)
    met()
    total = reduce_parts(me, acc_s, acc_t, got_s, got_t, sum_t, far_t, sem_s, sem_t)
    own[...] = emission_ref[y] + reflect_ref[y] * total

    def across(i):
        return remote(own, out_ref.at[y], sem_o, i, (x, (y + i) % NY, z, c))

    start_all(1, NY, across)
    out_ref[y] = own[...]
    wait_all(1, NY, across)


def sems(n):
    return pltpu.SemaphoreType.DMA((2, n))


def shape(dims, dtype=F32):
    return jax.ShapeDtypeStruct(dims, dtype)


def call(kernel, ident, inputs, outputs, scratch, name, specs=None, out_specs=None):
    params = {"vmem_limit_bytes": 60 * 1024 * 1024}
    if ident is not None:
        params.update(collective_id=ident, has_side_effects=True)
    return pl.pallas_call(
        kernel,
        out_shape=outputs,
        in_specs=specs or [VMEM] * len(inputs),
        out_specs=out_specs or [VMEM] * len(outputs),
        scratch_shapes=scratch,
        compiler_params=pltpu.CompilerParams(**params),
        name=name,
    )(*inputs)


ANY = pl.BlockSpec(memory_space=pl.ANY)


def pairs_call(first, lists, geo_s, geo_t, w_s, w_t, cache=None):
    outputs = [shape((16 * NS, 8, 256)), shape((4 * NT, 8, 256))]
    scratch = [pltpu.VMEM((16 * NS + 1, 8, 256), F32), pltpu.VMEM((4 * NT + 1, 8, 256), F32),
               pltpu.VMEM((16 * NS + 1, 8, 256), F32), pltpu.VMEM((4 * NT + 1, 8, 256), F32),
               pltpu.VMEM((2, 32, 128), F32)]
    depth = RING if first else DEPTH
    scratch += [pltpu.VMEM((depth, 2, 256, 256), BF16), pltpu.SemaphoreType.DMA((depth,))]
    if first:
        outputs += [shape((544,), I32), shape((PAIRS_KEPT, 2, 256, 256), BF16)]
        acc_s, acc_t, order, cache = call(
            pair_kernel, None, (lists, geo_s, geo_t, w_s, w_t), outputs, scratch, "pairs",
            [SMEM] + [VMEM] * 4, [VMEM, VMEM, SMEM, ANY],
        )
    else:
        acc_s, acc_t = call(
            again_kernel, None, (lists, geo_s, geo_t, w_s, w_t, cache), outputs, scratch, "again",
            [SMEM] + [VMEM] * 4 + [ANY],
        )
        order = lists
    return acc_s.reshape(4 * NS, 32, 256), acc_t.reshape(NT, 32, 256), order, cache


def shards(positions, facing, area, emission, reflect, pair_list):
    held = pair_list.reshape(128, 2)
    code = jnp.where(held[:, 0] >= 0, (held[:, 0] % 16) * 16 + held[:, 1] % 16, -1)
    code = jnp.broadcast_to(code[None, :], (8, 128))
    plane = NX * NY * NC
    geo_s, geo_t, w_s, w_t, lists = call(
        gather_kernel, 0, (positions, facing, area, emission, code),
        [shape((4 * NS, 24, 256)), shape((NT, 24, 256)), shape((4 * NS, 32, 256), BF16),
         shape((NT, 32, 256), BF16), shape((plane, 128), I32)],
        [pltpu.VMEM((4, 24, 256), F32), pltpu.VMEM((4, 32, 256), BF16), pltpu.VMEM((8, 128), I32),
         pltpu.VMEM((plane, 8, 128), I32), sems(LINE_GATHER), sems(LINE_GATHER), sems(NS), sems(NS), sems(plane)],
        "gather",
    )

    emission4, reflect4 = emission.reshape(4, 32, 256), reflect.reshape(4, 32, 256)
    landing = [pltpu.VMEM((plane, 32, 256), F32), pltpu.VMEM((15, 32, 256), F32),
               pltpu.VMEM((4, 32, 256), F32), pltpu.VMEM((4, 32, 256), F32)]
    acc_s, acc_t, order, cache = pairs_call(True, lists, geo_s, geo_t, w_s, w_t)
    w_s, w_t = call(
        turn_kernel, 1, (acc_s, acc_t, area, emission4, reflect4),
        [shape((4 * NS, 32, 256), BF16), shape((NT, 32, 256), BF16)],
        landing + [pltpu.VMEM((32, 256), BF16), sems(plane), sems(LINE_SUM), sems(plane), sems(LINE_GATHER)],
        "turn",
    )
    acc_s, acc_t, _, _ = pairs_call(False, order, geo_s, geo_t, w_s, w_t, cache)
    (out,) = call(
        last_kernel, 2, (acc_s, acc_t, emission4, reflect4), [shape((4, 32, 256))],
        landing + [pltpu.VMEM((32, 256), F32), sems(plane), sems(LINE_SUM), sems(NY)],
        "last",
    )
    return out.reshape(16, 8, 256)


def solution(mesh):
    placed = (
        P(None, "pairs", None),
        P(None, "pairs", None),
        P("pairs", None),
        P("pairs", None, None),
        P("pairs", None, None),
        P("pairs", "rep", None, None, None),
    )
    return jax.shard_map(
        shards, mesh=mesh, in_specs=placed, out_specs=P("pairs", None, None), check_vma=False
    )
```

```python
import functools
import math

import jax
import jax.numpy as jnp
from jax import lax
from jax.experimental import pallas as pl
from jax.experimental.pallas import tpu as pltpu
from jax.sharding import PartitionSpec as P

MESH = pl.DeviceIdType.MESH
VMEM = pl.BlockSpec(memory_space=pltpu.VMEM)
SMEM = pl.BlockSpec(memory_space=pltpu.SMEM)
HBM = pl.BlockSpec(memory_space=pltpu.HBM)
F32, BF16, I32 = jnp.float32, jnp.bfloat16, jnp.int32

NX, NY, NZ, NC = 4, 4, 16, 2
NS, NT = NX * NC, NZ
ROOT_PI = math.sqrt(math.pi)
SOFTEN = 0.1


def place():
    p = lax.axis_index("pairs")
    return p // (NZ * NC), lax.axis_index("rep"), (p // NC) % NZ, p % NC


def device(x, y, z, c):
    return {"pairs": (x * NZ + z) * NC + c, "rep": y}


def plane_peer(me, i):
    x, y, z, c = me
    return (x + i // NY) % NX, (y + i % NY) % NY, z, c


def plane_source(me, i):
    x, y, z, c = me
    return (x - i // NY + NX) % NX, (y - i % NY + NY) % NY, z, c


def sibling(me):
    return me[0], me[1], me[2], 1 - me[3]


def plane_slot(at):
    return (at[0] * NC + at[3]) * NY + at[1]


def line_peer(me, d):
    x, y, z, c = me
    return x, y, (z + d + NZ) % NZ, c


NEAR = (1, -1)
LINE = (1, -1, 2, -2, 3, -3)
PLANE = NX * NY


def greet(me):
    barrier = pltpu.get_barrier_semaphore()
    for d in LINE:
        pl.semaphore_signal(barrier, inc=1, device_id=device(*line_peer(me, d)), device_id_type=MESH)
    pl.semaphore_signal(barrier, inc=1, device_id=device(*sibling(me)), device_id_type=MESH)

    def plane(i, _):
        pl.semaphore_signal(barrier, inc=1, device_id=device(*plane_peer(me, i)), device_id_type=MESH)
        return 0

    lax.fori_loop(1, PLANE, plane, 0)


def met():
    pl.semaphore_wait(pltpu.get_barrier_semaphore(), PLANE + len(LINE))


def remote(src, dst, sems, i, peer):
    return pltpu.make_async_remote_copy(
        src_ref=src,
        dst_ref=dst,
        send_sem=sems.at[0, i],
        recv_sem=sems.at[1, i],
        device_id=device(*peer),
        device_id_type=MESH,
    )


def start_all(first, last, copy):
    def body(i, _):
        copy(i).start()
        return 0

    lax.fori_loop(first, last, body, 0)


def wait_all(first, last, copy):
    def body(i, _):
        copy(i).wait()
        return 0

    lax.fori_loop(first, last, body, 0)


def line_gather(me, own, into, sems):
    z = me[2]

    def start(source, block, step, n):
        copy = remote(block, into.at[source], sems, n, line_peer(me, step))
        copy.start()
        return copy

    first = [start(z, own, e, n) for n, e in enumerate((3, -3) + NEAR)]
    onward, others = [], []

    def spread(arrived, back, steps, n):
        arrived.wait_recv()
        source = (z + back + NZ) % NZ
        return [start(source, into.at[source], e, n + k) for k, e in enumerate(steps)]

    def from_three():
        for copy, back, n in ((first[0], -3, 4), (first[1], 3, 7)):
            copies = spread(copy, back, (-back,) + NEAR, n)
            onward.append(copies[0])
            others.extend(copies[1:])

    def from_six():
        others.extend(spread(onward[0], -6, NEAR, 10))
        others.extend(spread(onward[1], 6, NEAR + (-2,), 12))

    def end():
        for copy in first[2:] + others:
            copy.wait_recv()
        for copy in first + onward + others:
            copy.wait_send()

    return from_three, from_six, end


LINE_GATHER = 15


def plane_gather(me, own, into, sems):
    def across(i):
        return remote(own, into.at[plane_slot(me)], sems, i, plane_peer(me, i))

    def beside(i):
        block = into.at[plane_slot(plane_source(me, i))]
        return remote(block, block, sems, PLANE + i, sibling(me))

    direct = remote(own, into.at[plane_slot(me)], sems, PLANE, sibling(me))
    start_all(1, PLANE, across)
    direct.start()

    def relay():
        def pass_on(i, _):
            across(i).wait_recv()
            beside(i).start()
            return 0

        lax.fori_loop(1, PLANE, pass_on, 0)

    def end():
        def one(i, _):
            across(i).wait_send()
            beside(i).wait()
            return 0

        lax.fori_loop(1, PLANE, one, 0)
        direct.wait()

    return relay, end


PLANE_GATHER = 2 * PLANE


def gather_kernel(pos_hbm, facing_hbm, area_hbm, emission_hbm, code_ref,
                  geo_s, geo_t, w_s, w_t, lists_ref,
                  pos_ref, facing_ref, area_ref, emission_ref, sem_in,
                  own_geo, own_w, own_code, codes, sem_gt, sem_wt, sem_gs, sem_ws, sem_l):
    me = place()
    x, y, z, c = me
    mine = x * NC + c
    greet(me)
    loads = [pltpu.make_async_copy(source, target, sem_in.at[n])
             for n, (source, target) in enumerate(((facing_hbm, facing_ref), (pos_hbm, pos_ref),
                                                   (area_hbm, area_ref), (emission_hbm, emission_ref)))]
    for load in loads:
        load.start()
    for load in loads:
        load.wait()
    azimuth, elevation = facing_ref[0], facing_ref[1]
    flat = jnp.cos(elevation)
    parts = [pos_ref[0], pos_ref[1], pos_ref[2],
             jnp.cos(azimuth) * flat, jnp.sin(azimuth) * flat, jnp.sin(elevation)]
    for k in range(4):
        for comp in range(6):
            own_geo[k, comp * 4 : comp * 4 + 4, :] = parts[comp][4 * k : 4 * k + 4, :]
        own_w[k] = jnp.concatenate(
            [area_ref[4 * k + b : 4 * k + b + 1, :] * emission_ref[4 * k + b] for b in range(4)], axis=0
        ).astype(BF16)
    own_code[...] = code_ref[...]
    met()

    def across(own, into, sems, dx):
        return remote(own, into.at[pl.ds(4 * mine, 4)], sems, dx, ((x + dx) % NX, y, z, c))

    def beside(own, into, sems, dx):
        there = pl.ds(4 * (((x - dx + NX) % NX) * NC + c), 4)
        source = own if dx == 0 else into.at[there]
        return remote(source, into.at[there], sems, NX + dx, (x, y, z, 1 - c))

    plane = ((own_geo, geo_s, sem_gs), (own_w, w_s, sem_ws))
    line = (line_gather(me, own_geo.at[y], geo_t, sem_gt), line_gather(me, own_w.at[y], w_t, sem_wt))
    crossing = [across(*args, dx) for args in plane for dx in range(1, NX)]
    siblings = [beside(*args, dx) for args in plane for dx in range(NX)]
    for copy in crossing + [siblings[0], siblings[NX]]:
        copy.start()
    relay_lists, end_lists = plane_gather(me, own_code, codes, sem_l)
    geo_t[z] = own_geo[y]
    w_t[z] = own_w[y]
    geo_s[pl.ds(4 * mine, 4)] = own_geo[...]
    w_s[pl.ds(4 * mine, 4)] = own_w[...]
    codes[mine * NY + y] = own_code[...]
    for n in range(2):
        line[n][0]()
    for n in range(2):
        for dx in range(1, NX):
            crossing[n * (NX - 1) + dx - 1].wait_recv()
            siblings[n * NX + dx].start()
    relay_lists()
    for n in range(2):
        line[n][1]()
    end_lists()
    for s in range(NX * NY * NC):
        lists_ref[s : s + 1, :] = codes[s, 0:1, :]
    code = lists_ref[...]
    lane = lax.broadcasted_iota(I32, code.shape, 1)
    owner = lax.broadcasted_iota(I32, code.shape, 0) >> 2
    code = pltpu.roll(code, (128 - (x * (NZ * NC) + c)) & 127, 1)
    ours = (code >= 0) & (((code >> 2) & 3) == y)
    entry = (owner * 16 + (code >> 4)) | (((((lane & 31) >> 1) * 4) + (code & 3)) << 8)
    lists_ref[...] = jnp.where(ours, entry, -1)
    for copy in crossing:
        copy.wait_send()
    for copy in siblings:
        copy.wait()
    for steps in line:
        steps[2]()


def three(v):
    high = v.astype(BF16)
    rest = v - high.astype(F32)
    middle = rest.astype(BF16)
    return high, middle, (rest - middle.astype(F32)).astype(BF16)


AT_ONCE = 2
KEPT = 128 // AT_ONCE
UNUSED = (16 * NS) | ((4 * NT) << 8)


def unpack_geometry(q, geo, g, spread_geo):
    data = geo[q]
    product = data[0:12] * data[12:24]
    square = data[0:12] * data[0:12]
    product = product[0:4] + product[4:8] + product[8:12]
    square = square[0:4] + square[4:8] + square[8:12]
    for half in range(2):
        lanes = slice(128 * half, 128 * half + 128)
        spread_geo[half, 0:24, :] = data[:, lanes]
        spread_geo[half, 24:28, :] = product[:, lanes]
        spread_geo[half, 28:32, :] = square[:, lanes]
        for b in range(4):
            g[4 * q + b, :, lanes] = spread_geo[half, pl.ds(b, 8, stride=4), :]


def unpack_values(q, w, v):
    values = w[q].astype(F32)
    for b in range(4):
        v[4 * q + b] = values[8 * b : 8 * b + 8]


def clear_tail(*refs):
    for ref in refs:
        ref[ref.shape[0] - 1] = jnp.zeros((8, 256), F32)


def features(entry, g_s, g_t, left, right, k):
    gi, gj = g_s[entry & 255], g_t[entry >> 8]
    row = lax.broadcasted_iota(I32, (8, 256), 0)
    unit = jnp.where(row == 0, 1.0, 0.0).astype(F32)
    zero = jnp.zeros((8, 256), F32)
    h, m, l = three(jnp.concatenate([gi, unit], axis=0))
    left[k] = jnp.concatenate([h, h, m, h, l, m], axis=0).T
    near = jnp.where((row >= 3) & (row < 6), pltpu.roll(gj, 3, 0), jnp.where(row == 6, -1.0, 0.0))
    far = jnp.where(row < 3, pltpu.roll(gj, 5, 0), 0.0)
    far_low = jnp.where(row == 0, -pltpu.roll(gj, 2, 0), 0.0)
    dist = jnp.where(row < 3, (-2.0 * ROOT_PI) * gj, jnp.where(row == 7, ROOT_PI, 0.0))
    dist_low = jnp.where(row == 0, ROOT_PI * (pltpu.roll(gj, 1, 0) + SOFTEN), 0.0)
    for n, (top, low) in enumerate(((near, zero), (far, far_low), (dist, dist_low))):
        h, m, l = three(jnp.concatenate([top, low], axis=0))
        right[k, n] = jnp.concatenate([h, m, h, l, h, m], axis=0)


def couple(left, right, k):
    rows = left[k]
    near, far, dist = [jnp.dot(rows, right[k, n], preferred_element_type=F32) for n in range(3)]
    inverse = pl.reciprocal(dist, approx=False)
    return (jnp.maximum(near, 0.0) * jnp.maximum(far, 0.0) * (inverse * inverse)).astype(BF16)


def apply(entry, kernel, v_s, v_t, acc_s, acc_t):
    i, j = entry & 255, entry >> 8
    acc_s[i & (16 * NS - 1)] += lax.dot_general(
        v_t[j].astype(BF16), kernel, (((1,), (1,)), ((), ())), preferred_element_type=F32
    )
    acc_t[j & (4 * NT - 1)] += jnp.dot(v_s[i].astype(BF16), kernel, preferred_element_type=F32)


def pair_kernel(lists_ref, geo_s, geo_t, w_s, w_t, acc_s, acc_t, order, cache,
                g_s, g_t, v_s, v_t, spread_geo, left, right, held):
    x, y, z, c = place()
    acc_s[...] = jnp.zeros_like(acc_s)
    acc_t[...] = jnp.zeros_like(acc_t)
    clear_tail(g_s, g_t, v_s, v_t)

    def prepare_t(q, _):
        unpack_geometry(q, geo_t, g_t, spread_geo)
        unpack_values(q, w_t, v_t)
        return 0

    def prepare_s(q, count):
        unpack_geometry(q, geo_s, g_s, spread_geo)
        unpack_values(q, w_s, v_s)
        for zz in range(NZ):
            entry = lists_ref[q, zz * NC]
            order[count] = entry
            count = count + 1 + (entry >> 31)
        return count

    lax.fori_loop(0, NT, prepare_t, 0)
    count = lax.fori_loop(0, 4 * NS, prepare_s, jnp.int32(1))
    for k in range(2 * AT_ONCE):
        order[count + k] = jnp.int32(UNUSED)
    order[0] = count - 1
    turns = (count + AT_ONCE - 2) // AT_ONCE
    held[...] = jnp.zeros_like(held)
    for k in range(AT_ONCE):
        features(order[1 + k], g_s, g_t, left, right, k)

    def turn(t, last):
        now = tuple(order[AT_ONCE * t + 1 + k] for k in range(AT_ONCE))
        kept = jnp.minimum(t, KEPT)
        for k in range(AT_ONCE):
            apply(last[k], held[k], v_s, v_t, acc_s, acc_t)
        for k in range(AT_ONCE):
            kernel = couple(left, right, k)
            held[k] = kernel
            cache[kept, k] = kernel
        for k in range(AT_ONCE):
            features(order[AT_ONCE * (t + 1) + 1 + k], g_s, g_t, left, right, k)
        return now

    last = lax.fori_loop(0, turns, turn, (jnp.int32(UNUSED),) * AT_ONCE)
    for k in range(AT_ONCE):
        apply(last[k], held[k], v_s, v_t, acc_s, acc_t)


def again_kernel(order, geo_s, geo_t, w_s, w_t, cache, acc_s, acc_t,
                 g_s, g_t, v_s, v_t, spread_geo, left, right):
    turns = (order[0] + AT_ONCE - 1) // AT_ONCE
    acc_s[...] = jnp.zeros_like(acc_s)
    acc_t[...] = jnp.zeros_like(acc_t)
    clear_tail(g_s, g_t, v_s, v_t)

    def prepare_s(q, _):
        unpack_values(q, w_s, v_s)
        return 0

    def prepare_t(q, _):
        unpack_values(q, w_t, v_t)
        return 0

    lax.fori_loop(0, 4 * NS, prepare_s, 0)
    lax.fori_loop(0, NT, prepare_t, 0)

    def turn(t, _):
        for k in range(AT_ONCE):
            apply(order[AT_ONCE * t + 1 + k], cache[t, k], v_s, v_t, acc_s, acc_t)
        return 0

    lax.fori_loop(0, jnp.minimum(turns, KEPT), turn, 0)

    @pl.when(turns > KEPT)
    def _():
        def shape_s(q, _):
            unpack_geometry(q, geo_s, g_s, spread_geo)
            return 0

        def shape_t(q, _):
            unpack_geometry(q, geo_t, g_t, spread_geo)
            return 0

        def more(t, _):
            entry = order[t]
            features(entry, g_s, g_t, left, right, 0)
            apply(entry, couple(left, right, 0), v_s, v_t, acc_s, acc_t)
            return 0

        lax.fori_loop(0, 4 * NS, shape_s, 0)
        lax.fori_loop(0, NT, shape_t, 0)
        lax.fori_loop(AT_ONCE * KEPT + 1, AT_ONCE * turns + 1, more, 0)


def reduce_parts(me, acc_s, acc_t, half_s, sum_s, got_s, got_t, sum_t, far_t, sem_h, sem_s, sem_t):
    x, y, z, c = me

    def halves(n):
        return remote(acc_s.at[pl.ds((n * NC + 1 - c) * NY, NY)], half_s.at[n], sem_h, n, sibling(me))

    def plane(i):
        peer = plane_peer(me, i)
        return remote(sum_s.at[peer[0] * NY + peer[1]], got_s.at[i], sem_s, i, peer)

    def toward(n, h, k, e):
        piece = acc_t.at[(z + e - h + NZ) % NZ]
        return remote(piece, got_t.at[3 * n + k], sem_t, 3 * n + k, line_peer(me, e))

    start_all(0, NX, halves)
    hubs = (6, -6, 3, -3, 0)
    near = [[toward(n, h, k, e) for k, e in enumerate(NEAR + (2,) if h == -6 else NEAR)]
            for n, h in enumerate(hubs)]
    for copies in near:
        for copy in copies:
            copy.start()
    for n in range(NX):
        halves(n).wait_recv()
        sum_s[n * NY : n * NY + NY] = acc_s[pl.ds((n * NC + c) * NY, NY)] + half_s[n]
    start_all(1, PLANE, plane)
    far = []
    for n, h in enumerate(hubs):
        part = acc_t[(z - h + NZ) % NZ]
        for k, copy in enumerate(near[n]):
            copy.wait_recv()
            part = part + got_t[3 * n + k]
        if abs(h) == 3:
            far[n - 2].wait_recv()
            part = part + far_t[n - 2]
        if h:
            sum_t[n] = part
            far.append(remote(sum_t.at[n], far_t.at[n], sem_t, 15 + n, line_peer(me, -3 if h > 0 else 3)))
            far[n].start()
    total = part + sum_s[x * NY + y]
    wait_all(1, PLANE, plane)
    total = lax.fori_loop(1, PLANE, lambda i, t: t + got_s[i], total)
    for n in (2, 3):
        far[n].wait_recv()
        total = total + far_t[n]
    for n in range(NX):
        halves(n).wait_send()
    for copies in near:
        for copy in copies:
            copy.wait_send()
    for copy in far:
        copy.wait_send()
    return total


LINE_SUM = 19


def turn_kernel(acc_s, acc_t, emission_hbm, reflect_hbm, area_hbm, w_s, w_t,
                emission_ref, reflect_ref, area_ref, sem_in,
                half_s, sum_s, got_s, got_t, sum_t, far_t, own_w,
                sem_h, sem_s, sem_t, sem_ws, sem_wt):
    me = place()
    x, y, z, c = me
    greet(me)
    loads = [pltpu.make_async_copy(source, target, sem_in.at[n])
             for n, (source, target) in enumerate(((emission_hbm.at[y], emission_ref),
                                                   (reflect_hbm.at[y], reflect_ref), (area_hbm, area_ref)))]
    for load in loads:
        load.start()
    met()
    total = reduce_parts(
        me, acc_s, acc_t, half_s, sum_s, got_s, got_t, sum_t, far_t, sem_h, sem_s, sem_t
    )
    for load in loads:
        load.wait()
    radiosity = emission_ref[...] + reflect_ref[...] * total
    area = jnp.concatenate(
        [jnp.broadcast_to(area_ref[pl.ds(4 * y + b, 1), :], (8, 256)) for b in range(4)], axis=0
    )
    own_w[...] = (area * radiosity).astype(BF16)
    from_three, from_six, end_line = line_gather(me, own_w, w_t, sem_wt)
    relay, end_plane = plane_gather(me, own_w, w_s, sem_ws)
    w_t[z] = own_w[...]
    w_s[plane_slot(me)] = own_w[...]
    from_three()
    relay()
    from_six()
    end_plane()
    end_line()


def last_kernel(acc_s, acc_t, emission_hbm, reflect_hbm, out_ref,
                emission_ref, reflect_ref, sem_in,
                half_s, sum_s, got_s, got_t, sum_t, far_t, own,
                sem_h, sem_s, sem_t, sem_o):
    me = place()
    x, y, z, c = me
    greet(me)
    loads = [pltpu.make_async_copy(source, target, sem_in.at[n])
             for n, (source, target) in enumerate(((emission_hbm.at[y], emission_ref),
                                                   (reflect_hbm.at[y], reflect_ref)))]
    for load in loads:
        load.start()
    met()
    total = reduce_parts(
        me, acc_s, acc_t, half_s, sum_s, got_s, got_t, sum_t, far_t, sem_h, sem_s, sem_t
    )
    for load in loads:
        load.wait()
    own[...] = emission_ref[...] + reflect_ref[...] * total

    def across(i):
        return remote(own, out_ref.at[y], sem_o, i, (x, (y + i) % NY, z, c))

    start_all(1, NY, across)
    out_ref[y] = own[...]
    wait_all(1, NY, across)


def sems(n):
    return pltpu.SemaphoreType.DMA((2, n))


def shape(dims, dtype=F32):
    return jax.ShapeDtypeStruct(dims, dtype)


def call(kernel, ident, inputs, outputs, scratch, name, specs=None, out_specs=None, mib=10):
    params = {"vmem_limit_bytes": mib * 1024 * 1024}
    if ident is None:
        params.update()
    else:
        params.update(collective_id=ident, has_side_effects=True)
    return pl.pallas_call(
        kernel,
        out_shape=outputs,
        in_specs=specs or [VMEM] * len(inputs),
        out_specs=out_specs or [VMEM] * len(outputs),
        scratch_shapes=scratch,
        compiler_params=pltpu.CompilerParams(**params),
        name=name,
    )(*inputs)


PAIR_MIB = 24


def pairs_call(first, lists, geo_s, geo_t, w_s, w_t, cache=None):
    outputs = [shape((16 * NS, 8, 256)), shape((4 * NT, 8, 256))]
    scratch = [pltpu.VMEM((16 * NS + 1, 8, 256), F32), pltpu.VMEM((4 * NT + 1, 8, 256), F32),
               pltpu.VMEM((16 * NS + 1, 8, 256), F32), pltpu.VMEM((4 * NT + 1, 8, 256), F32),
               pltpu.VMEM((2, 32, 128), F32)]
    scratch += [pltpu.VMEM((AT_ONCE, 256, 96), BF16), pltpu.VMEM((AT_ONCE, 3, 96, 256), BF16)]
    if first:
        scratch += [pltpu.VMEM((AT_ONCE, 256, 256), BF16)]
        outputs += [shape((544,), I32), shape((KEPT + 1, AT_ONCE, 256, 256), BF16)]
        acc_s, acc_t, order, cache = call(
            pair_kernel, None, (lists, geo_s, geo_t, w_s, w_t), outputs, scratch, "pairs",
            [SMEM] + [VMEM] * 4, [VMEM, VMEM, SMEM, VMEM], PAIR_MIB,
        )
    else:
        acc_s, acc_t = call(
            again_kernel, None, (lists, geo_s, geo_t, w_s, w_t, cache), outputs, scratch, "again",
            [SMEM] + [VMEM] * 5, None, PAIR_MIB,
        )
        order = lists
    return acc_s.reshape(4 * NS, 32, 256), acc_t.reshape(NT, 32, 256), order, cache


def stay(x):
    return pltpu.with_memory_space_constraint(x, pltpu.HBM)


def shards(positions, facing, area, emission, reflect, pair_list):
    held = pair_list.reshape(128, 2)
    emission4, reflect4 = stay(emission.reshape(4, 32, 256)), stay(reflect.reshape(4, 32, 256))
    positions, facing, area, emission = stay(positions), stay(facing), stay(area), stay(emission)
    code = jnp.where(held[:, 0] >= 0, (held[:, 0] % 16) * 16 + held[:, 1] % 16, -1)
    code = jnp.broadcast_to(code[None, :], (8, 128))
    plane = NX * NY * NC
    geo_s, geo_t, w_s, w_t, lists = call(
        gather_kernel, 0, (positions, facing, area, emission, code),
        [shape((4 * NS, 24, 256)), shape((NT, 24, 256)), shape((4 * NS, 32, 256), BF16),
         shape((NT, 32, 256), BF16), shape((plane, 128), I32)],
        [pltpu.VMEM((3, 16, 256), F32), pltpu.VMEM((2, 16, 256), F32), pltpu.VMEM((16, 256), F32),
         pltpu.VMEM((16, 8, 256), F32), pltpu.SemaphoreType.DMA((4,)),
         pltpu.VMEM((4, 24, 256), F32), pltpu.VMEM((4, 32, 256), BF16), pltpu.VMEM((8, 128), I32),
         pltpu.VMEM((plane, 8, 128), I32), sems(LINE_GATHER), sems(LINE_GATHER), sems(NS), sems(NS), sems(PLANE_GATHER)],
        "gather", [HBM] * 4 + [VMEM],
    )

    quarter = pltpu.VMEM((32, 256), F32)
    landing = [pltpu.VMEM((NX, NY, 32, 256), F32), pltpu.VMEM((PLANE, 32, 256), F32),
               pltpu.VMEM((PLANE, 32, 256), F32), pltpu.VMEM((15, 32, 256), F32),
               pltpu.VMEM((4, 32, 256), F32), pltpu.VMEM((4, 32, 256), F32)]
    acc_s, acc_t, order, cache = pairs_call(True, lists, geo_s, geo_t, w_s, w_t)
    w_s, w_t = call(
        turn_kernel, 1, (acc_s, acc_t, emission4, reflect4, area),
        [shape((4 * NS, 32, 256), BF16), shape((NT, 32, 256), BF16)],
        [quarter, quarter, pltpu.VMEM((16, 256), F32), pltpu.SemaphoreType.DMA((3,))]
        + landing + [pltpu.VMEM((32, 256), BF16), sems(NX), sems(PLANE), sems(LINE_SUM),
                   sems(PLANE_GATHER), sems(LINE_GATHER)],
        "turn", [VMEM, VMEM, HBM, HBM, HBM],
    )
    acc_s, acc_t, _, _ = pairs_call(False, order, geo_s, geo_t, w_s, w_t, cache)
    (out,) = call(
        last_kernel, 2, (acc_s, acc_t, emission4, reflect4), [shape((4, 32, 256))],
        [quarter, quarter, pltpu.SemaphoreType.DMA((2,))] + landing + [pltpu.VMEM((32, 256), F32), sems(NX), sems(PLANE), sems(LINE_SUM), sems(NY)],
        "last", [VMEM, VMEM, HBM, HBM],
    )
    return out.reshape(16, 8, 256)


def solution(mesh):
    placed = (
        P(None, "pairs", None),
        P(None, "pairs", None),
        P("pairs", None),
        P("pairs", None, None),
        P("pairs", None, None),
        P("pairs", "rep", None, None, None),
    )
    return jax.shard_map(
        shards, mesh=mesh, in_specs=placed, out_specs=P("pairs", None, None), check_vma=False
    )
```

```python
import functools
import math

import jax
import jax.numpy as jnp
from jax import lax
from jax.experimental import pallas as pl
from jax.experimental.pallas import tpu as pltpu
from jax.sharding import PartitionSpec as P

MESH = pl.DeviceIdType.MESH
VMEM = pl.BlockSpec(memory_space=pltpu.VMEM)
SMEM = pl.BlockSpec(memory_space=pltpu.SMEM)
HBM = pl.BlockSpec(memory_space=pltpu.HBM)
F32, BF16, I32 = jnp.float32, jnp.bfloat16, jnp.int32

NX, NY, NZ, NC = 4, 4, 16, 2
NS, NT = NX * NC, NZ
ROOT_PI = math.sqrt(math.pi)
SOFTEN = 0.1


def place():
    p = lax.axis_index("pairs")
    return p // (NZ * NC), lax.axis_index("rep"), (p // NC) % NZ, p % NC


def device(x, y, z, c):
    return {"pairs": (x * NZ + z) * NC + c, "rep": y}


def plane_peer(me, i):
    x, y, z, c = me
    return (x + i // NY) % NX, (y + i % NY) % NY, z, c


def plane_source(me, i):
    x, y, z, c = me
    return (x - i // NY + NX) % NX, (y - i % NY + NY) % NY, z, c


def sibling(me):
    return me[0], me[1], me[2], 1 - me[3]


def plane_slot(at):
    return (at[0] * NC + at[3]) * NY + at[1]


def line_peer(me, d):
    x, y, z, c = me
    return x, y, (z + d + NZ) % NZ, c


NEAR = (1, -1)
LINE = (1, -1, 2, -2, 3, -3)
LINE_SHORT = LINE + (4, -4)
PLANE = NX * NY


def greet(me, line=LINE):
    barrier = pltpu.get_barrier_semaphore()
    for d in line:
        pl.semaphore_signal(barrier, inc=1, device_id=device(*line_peer(me, d)), device_id_type=MESH)
    pl.semaphore_signal(barrier, inc=1, device_id=device(*sibling(me)), device_id_type=MESH)

    def plane(i, _):
        pl.semaphore_signal(barrier, inc=1, device_id=device(*plane_peer(me, i)), device_id_type=MESH)
        return 0

    lax.fori_loop(1, PLANE, plane, 0)


def met(line=LINE):
    pl.semaphore_wait(pltpu.get_barrier_semaphore(), PLANE + len(line))


def remote(src, dst, sems, i, peer):
    return pltpu.make_async_remote_copy(
        src_ref=src,
        dst_ref=dst,
        send_sem=sems.at[0, i],
        recv_sem=sems.at[1, i],
        device_id=device(*peer),
        device_id_type=MESH,
    )


def start_all(first, last, copy):
    def body(i, _):
        copy(i).start()
        return 0

    lax.fori_loop(first, last, body, 0)


def wait_all(first, last, copy):
    def body(i, _):
        copy(i).wait()
        return 0

    lax.fori_loop(first, last, body, 0)


def line_gather(me, own, into, sems):
    z = me[2]

    def start(source, block, step, n):
        copy = remote(block, into.at[source], sems, n, line_peer(me, step))
        copy.start()
        return copy

    first = [start(z, own, e, n) for n, e in enumerate((3, -3) + NEAR)]
    onward, others = [], []

    def spread(arrived, back, steps, n):
        arrived.wait_recv()
        source = (z + back + NZ) % NZ
        return [start(source, into.at[source], e, n + k) for k, e in enumerate(steps)]

    def from_three():
        for copy, back, n in ((first[0], -3, 4), (first[1], 3, 7)):
            copies = spread(copy, back, (-back,) + NEAR, n)
            onward.append(copies[0])
            others.extend(copies[1:])

    def from_six():
        others.extend(spread(onward[0], -6, NEAR, 10))
        others.extend(spread(onward[1], 6, NEAR + (-2,), 12))

    def end():
        for copy in first[2:] + others:
            copy.wait_recv()
        for copy in first + onward + others:
            copy.wait_send()

    return from_three, from_six, end


LINE_GATHER = 15


def line_gather_short(me, own, into, sems):
    z = me[2]

    def start(source, block, step, n):
        copy = remote(block, into.at[source], sems, n, line_peer(me, step))
        copy.start()
        return copy

    first = [start(z, own, e, n) for n, e in enumerate((4, -4, 3, -3, 2, -2, 1, -1))]
    others = []

    def from_four():
        n = len(first)
        for arrived, back, steps in ((first[0], -4, (4, 3, 2, 1)), (first[1], 4, (-3, -2, -1))):
            arrived.wait_recv()
            source = (z + back + NZ) % NZ
            for e in steps:
                others.append(start(source, into.at[source], e, n))
                n += 1

    def end():
        for copy in first[2:] + others:
            copy.wait_recv()
        for copy in first + others:
            copy.wait_send()

    return from_four, end


def plane_gather(me, own, into, sems):
    def across(i):
        return remote(own, into.at[plane_slot(me)], sems, i, plane_peer(me, i))

    def beside(i):
        block = into.at[plane_slot(plane_source(me, i))]
        return remote(block, block, sems, PLANE + i, sibling(me))

    direct = remote(own, into.at[plane_slot(me)], sems, PLANE, sibling(me))
    start_all(1, PLANE, across)
    direct.start()

    def relay():
        def pass_on(i, _):
            across(i).wait_recv()
            beside(i).start()
            return 0

        lax.fori_loop(1, PLANE, pass_on, 0)

    def end():
        def one(i, _):
            across(i).wait_send()
            beside(i).wait()
            return 0

        lax.fori_loop(1, PLANE, one, 0)
        direct.wait()

    return relay, end


PLANE_GATHER = 2 * PLANE


def gather_kernel(pos_hbm, facing_hbm, area_hbm, emission_hbm, list_hbm,
                  geo_s, geo_t, w_s, w_t, lists_ref,
                  pos_ref, facing_ref, area_ref, emission_ref, list_ref, sem_in,
                  own_geo, own_w, own_code, codes, sem_gt, sem_wt, sem_gs, sem_ws, sem_l):
    me = place()
    x, y, z, c = me
    mine = x * NC + c
    greet(me)
    loads = [pltpu.make_async_copy(source, target, sem_in.at[n])
             for n, (source, target) in enumerate(((facing_hbm, facing_ref), (pos_hbm, pos_ref),
                                                   (area_hbm, area_ref), (emission_hbm, emission_ref),
                                                   (list_hbm, list_ref)))]
    for load in loads:
        load.start()
    for load in loads:
        load.wait()
    azimuth, elevation = facing_ref[0], facing_ref[1]
    flat = jnp.cos(elevation)
    parts = [pos_ref[0], pos_ref[1], pos_ref[2],
             jnp.cos(azimuth) * flat, jnp.sin(azimuth) * flat, jnp.sin(elevation)]
    for k in range(4):
        for comp in range(6):
            own_geo[k, comp * 4 : comp * 4 + 4, :] = parts[comp][4 * k : 4 * k + 4, :]
        own_w[k] = jnp.concatenate(
            [area_ref[4 * k + b : 4 * k + b + 1, :] * emission_ref[4 * k + b] for b in range(4)], axis=0
        ).astype(BF16)
    rows, columns = list_ref[0:1, :], list_ref[1:2, :]
    code = jnp.where(rows >= 0, (rows & 15) * 16 + (columns & 15), -1)
    own_code[...] = jnp.broadcast_to(code, (8, 128))
    met()

    def across(own, into, sems, dx):
        return remote(own, into.at[pl.ds(4 * mine, 4)], sems, dx, ((x + dx) % NX, y, z, c))

    def beside(own, into, sems, dx):
        there = pl.ds(4 * (((x - dx + NX) % NX) * NC + c), 4)
        source = own if dx == 0 else into.at[there]
        return remote(source, into.at[there], sems, NX + dx, (x, y, z, 1 - c))

    plane = ((own_geo, geo_s, sem_gs), (own_w, w_s, sem_ws))
    line = (line_gather(me, own_geo.at[y], geo_t, sem_gt), line_gather(me, own_w.at[y], w_t, sem_wt))
    crossing = [across(*args, dx) for args in plane for dx in range(1, NX)]
    siblings = [beside(*args, dx) for args in plane for dx in range(NX)]
    for copy in crossing + [siblings[0], siblings[NX]]:
        copy.start()
    relay_lists, end_lists = plane_gather(me, own_code, codes, sem_l)
    geo_t[z] = own_geo[y]
    w_t[z] = own_w[y]
    geo_s[pl.ds(4 * mine, 4)] = own_geo[...]
    w_s[pl.ds(4 * mine, 4)] = own_w[...]
    codes[mine * NY + y] = own_code[...]
    for n in range(2):
        line[n][0]()
    for n in range(2):
        for dx in range(1, NX):
            crossing[n * (NX - 1) + dx - 1].wait_recv()
            siblings[n * NX + dx].start()
    relay_lists()
    for n in range(2):
        line[n][1]()
    end_lists()
    for s in range(NX * NY * NC):
        lists_ref[s : s + 1, :] = codes[s, 0:1, :]
    code = lists_ref[...]
    lane = lax.broadcasted_iota(I32, code.shape, 1)
    owner = lax.broadcasted_iota(I32, code.shape, 0) >> 2
    code = pltpu.roll(code, (128 - (x * (NZ * NC) + c)) & 127, 1)
    ours = (code >= 0) & (((code >> 2) & 3) == y)
    entry = (owner * 16 + (code >> 4)) | (((((lane & 31) >> 1) * 4) + (code & 3)) << 8)
    lists_ref[...] = jnp.where(ours, entry, -1)
    for copy in crossing:
        copy.wait_send()
    for copy in siblings:
        copy.wait()
    for steps in line:
        steps[2]()


def three(v):
    high = v.astype(BF16)
    rest = v - high.astype(F32)
    middle = rest.astype(BF16)
    return high, middle, (rest - middle.astype(F32)).astype(BF16)


AT_ONCE = 2
KEPT = 128 // AT_ONCE
UNUSED = (16 * NS) | ((4 * NT) << 8)


def unpack_geometry(q, geo, g, spread_geo):
    data = geo[q]
    product = data[0:12] * data[12:24]
    square = data[0:12] * data[0:12]
    product = product[0:4] + product[4:8] + product[8:12]
    square = square[0:4] + square[4:8] + square[8:12]
    for half in range(2):
        lanes = slice(128 * half, 128 * half + 128)
        spread_geo[half, 0:24, :] = data[:, lanes]
        spread_geo[half, 24:28, :] = product[:, lanes]
        spread_geo[half, 28:32, :] = square[:, lanes]
        for b in range(4):
            g[4 * q + b, :, lanes] = spread_geo[half, pl.ds(b, 8, stride=4), :]


def unpack_values(q, w, v):
    values = w[q].astype(F32)
    for b in range(4):
        v[4 * q + b] = values[8 * b : 8 * b + 8]


def clear_tail(*refs):
    for ref in refs:
        ref[ref.shape[0] - 1] = jnp.zeros((8, 256), F32)


def features(entry, g_s, g_t, left, right, k):
    gi, gj = g_s[entry & 255], g_t[entry >> 8]
    row = lax.broadcasted_iota(I32, (8, 256), 0)
    unit = jnp.where(row == 0, 1.0, 0.0).astype(F32)
    zero = jnp.zeros((8, 256), F32)
    h, m, l = three(jnp.concatenate([gi, unit], axis=0))
    left[k] = jnp.concatenate([h, h, m, h, l, m], axis=0).T
    near = jnp.where((row >= 3) & (row < 6), pltpu.roll(gj, 3, 0), jnp.where(row == 6, -1.0, 0.0))
    far = jnp.where(row < 3, pltpu.roll(gj, 5, 0), 0.0)
    far_low = jnp.where(row == 0, -pltpu.roll(gj, 2, 0), 0.0)
    dist = jnp.where(row < 3, (-2.0 * ROOT_PI) * gj, jnp.where(row == 7, ROOT_PI, 0.0))
    dist_low = jnp.where(row == 0, ROOT_PI * (pltpu.roll(gj, 1, 0) + SOFTEN), 0.0)
    for n, (top, low) in enumerate(((near, zero), (far, far_low), (dist, dist_low))):
        h, m, l = three(jnp.concatenate([top, low], axis=0))
        right[k, n] = jnp.concatenate([h, m, h, l, h, m], axis=0)


def couple(left, right, k):
    rows = left[k]
    near, far, dist = [jnp.dot(rows, right[k, n], preferred_element_type=F32) for n in range(3)]
    inverse = pl.reciprocal(dist, approx=False)
    return (jnp.maximum(near, 0.0) * jnp.maximum(far, 0.0) * (inverse * inverse)).astype(BF16)


def apply(entry, kernel, v_s, v_t, acc_s, acc_t):
    i, j = entry & 255, entry >> 8
    acc_s[i & (16 * NS - 1)] += lax.dot_general(
        v_t[j].astype(BF16), kernel, (((1,), (1,)), ((), ())), preferred_element_type=F32
    )
    acc_t[j & (4 * NT - 1)] += jnp.dot(v_s[i].astype(BF16), kernel, preferred_element_type=F32)


def pair_kernel(lists_ref, geo_s, geo_t, w_s, w_t, acc_s, acc_t, order, cache,
                g_s, g_t, v_s, v_t, spread_geo, left, right, held):
    x, y, z, c = place()
    acc_s[...] = jnp.zeros_like(acc_s)
    acc_t[...] = jnp.zeros_like(acc_t)
    clear_tail(g_s, g_t, v_s, v_t)

    def prepare_t(q, _):
        unpack_geometry(q, geo_t, g_t, spread_geo)
        unpack_values(q, w_t, v_t)
        return 0

    def prepare_s(q, count):
        unpack_geometry(q, geo_s, g_s, spread_geo)
        unpack_values(q, w_s, v_s)
        for zz in range(NZ):
            entry = lists_ref[q, zz * NC]
            order[count] = entry
            count = count + 1 + (entry >> 31)
        return count

    lax.fori_loop(0, NT, prepare_t, 0)
    count = lax.fori_loop(0, 4 * NS, prepare_s, jnp.int32(1))
    for k in range(2 * AT_ONCE):
        order[count + k] = jnp.int32(UNUSED)
    order[0] = count - 1
    turns = (count + AT_ONCE - 2) // AT_ONCE
    held[...] = jnp.zeros_like(held)
    for k in range(AT_ONCE):
        features(order[1 + k], g_s, g_t, left, right, k)

    def turn(t, last):
        now = tuple(order[AT_ONCE * t + 1 + k] for k in range(AT_ONCE))
        kept = jnp.minimum(t, KEPT)
        for k in range(AT_ONCE):
            apply(last[k], held[k], v_s, v_t, acc_s, acc_t)
        for k in range(AT_ONCE):
            kernel = couple(left, right, k)
            held[k] = kernel
            cache[kept, k] = kernel
        for k in range(AT_ONCE):
            features(order[AT_ONCE * (t + 1) + 1 + k], g_s, g_t, left, right, k)
        return now

    last = lax.fori_loop(0, turns, turn, (jnp.int32(UNUSED),) * AT_ONCE)
    for k in range(AT_ONCE):
        apply(last[k], held[k], v_s, v_t, acc_s, acc_t)


def again_kernel(order, geo_s, geo_t, w_s, w_t, cache, acc_s, acc_t,
                 g_s, g_t, v_s, v_t, spread_geo, left, right):
    turns = (order[0] + AT_ONCE - 1) // AT_ONCE
    acc_s[...] = jnp.zeros_like(acc_s)
    acc_t[...] = jnp.zeros_like(acc_t)
    clear_tail(g_s, g_t, v_s, v_t)

    def prepare_s(q, _):
        unpack_values(q, w_s, v_s)
        return 0

    def prepare_t(q, _):
        unpack_values(q, w_t, v_t)
        return 0

    lax.fori_loop(0, 4 * NS, prepare_s, 0)
    lax.fori_loop(0, NT, prepare_t, 0)

    def turn(t, _):
        for k in range(AT_ONCE):
            apply(order[AT_ONCE * t + 1 + k], cache[t, k], v_s, v_t, acc_s, acc_t)
        return 0

    lax.fori_loop(0, jnp.minimum(turns, KEPT), turn, 0)

    @pl.when(turns > KEPT)
    def _():
        def shape_s(q, _):
            unpack_geometry(q, geo_s, g_s, spread_geo)
            return 0

        def shape_t(q, _):
            unpack_geometry(q, geo_t, g_t, spread_geo)
            return 0

        def more(t, _):
            entry = order[t]
            features(entry, g_s, g_t, left, right, 0)
            apply(entry, couple(left, right, 0), v_s, v_t, acc_s, acc_t)
            return 0

        lax.fori_loop(0, 4 * NS, shape_s, 0)
        lax.fori_loop(0, NT, shape_t, 0)
        lax.fori_loop(AT_ONCE * KEPT + 1, AT_ONCE * turns + 1, more, 0)


def reduce_parts(me, acc_s, acc_t, half_s, sum_s, got_s, got_t, sum_t, far_t, sem_h, sem_s, sem_t):
    x, y, z, c = me

    def halves(n):
        return remote(acc_s.at[pl.ds((n * NC + 1 - c) * NY, NY)], half_s.at[n], sem_h, n, sibling(me))

    def plane(i):
        peer = plane_peer(me, i)
        return remote(sum_s.at[peer[0] * NY + peer[1]], got_s.at[i], sem_s, i, peer)

    def toward(n, h, k, e):
        piece = acc_t.at[(z + e - h + NZ) % NZ]
        return remote(piece, got_t.at[3 * n + k], sem_t, 3 * n + k, line_peer(me, e))

    start_all(0, NX, halves)
    hubs = (6, -6, 3, -3, 0)
    near = [[toward(n, h, k, e) for k, e in enumerate(NEAR + (2,) if h == -6 else NEAR)]
            for n, h in enumerate(hubs)]
    for copies in near:
        for copy in copies:
            copy.start()
    for n in range(NX):
        halves(n).wait_recv()
        sum_s[n * NY : n * NY + NY] = acc_s[pl.ds((n * NC + c) * NY, NY)] + half_s[n]
    start_all(1, PLANE, plane)
    far = []
    for n, h in enumerate(hubs):
        part = acc_t[(z - h + NZ) % NZ]
        for k, copy in enumerate(near[n]):
            copy.wait_recv()
            part = part + got_t[3 * n + k]
        if abs(h) == 3:
            far[n - 2].wait_recv()
            part = part + far_t[n - 2]
        if h:
            sum_t[n] = part
            far.append(remote(sum_t.at[n], far_t.at[n], sem_t, 15 + n, line_peer(me, -3 if h > 0 else 3)))
            far[n].start()
    total = part + sum_s[x * NY + y]
    wait_all(1, PLANE, plane)
    total = lax.fori_loop(1, PLANE, lambda i, t: t + got_s[i], total)
    for n in (2, 3):
        far[n].wait_recv()
        total = total + far_t[n]
    for n in range(NX):
        halves(n).wait_send()
    for copies in near:
        for copy in copies:
            copy.wait_send()
    for copy in far:
        copy.wait_send()
    return total


LINE_SUM = 19


def turn_kernel(acc_s, acc_t, emission_hbm, reflect_hbm, area_hbm, w_s, w_t,
                emission_ref, reflect_ref, area_ref, sem_in,
                half_s, sum_s, got_s, got_t, sum_t, far_t, own_w,
                sem_h, sem_s, sem_t, sem_ws, sem_wt):
    me = place()
    x, y, z, c = me
    greet(me, LINE_SHORT)
    loads = [pltpu.make_async_copy(source, target, sem_in.at[n])
             for n, (source, target) in enumerate(((emission_hbm.at[y], emission_ref),
                                                   (reflect_hbm.at[y], reflect_ref), (area_hbm, area_ref)))]
    for load in loads:
        load.start()
    met(LINE_SHORT)
    total = reduce_parts(
        me, acc_s, acc_t, half_s, sum_s, got_s, got_t, sum_t, far_t, sem_h, sem_s, sem_t
    )
    for load in loads:
        load.wait()
    radiosity = emission_ref[...] + reflect_ref[...] * total
    area = jnp.concatenate(
        [jnp.broadcast_to(area_ref[pl.ds(4 * y + b, 1), :], (8, 256)) for b in range(4)], axis=0
    )
    own_w[...] = (area * radiosity).astype(BF16)
    from_four, end_line = line_gather_short(me, own_w, w_t, sem_wt)
    relay, end_plane = plane_gather(me, own_w, w_s, sem_ws)
    w_t[z] = own_w[...]
    w_s[plane_slot(me)] = own_w[...]
    relay()
    from_four()
    end_plane()
    end_line()


def last_kernel(acc_s, acc_t, emission_hbm, reflect_hbm, out_ref,
                emission_ref, reflect_ref, sem_in,
                half_s, sum_s, got_s, got_t, sum_t, far_t, own,
                sem_h, sem_s, sem_t, sem_o):
    me = place()
    x, y, z, c = me
    greet(me)
    loads = [pltpu.make_async_copy(source, target, sem_in.at[n])
             for n, (source, target) in enumerate(((emission_hbm.at[y], emission_ref),
                                                   (reflect_hbm.at[y], reflect_ref)))]
    for load in loads:
        load.start()
    met()
    total = reduce_parts(
        me, acc_s, acc_t, half_s, sum_s, got_s, got_t, sum_t, far_t, sem_h, sem_s, sem_t
    )
    for load in loads:
        load.wait()
    own[...] = emission_ref[...] + reflect_ref[...] * total

    def across(i):
        return remote(own, out_ref.at[y], sem_o, i, (x, (y + i) % NY, z, c))

    start_all(1, NY, across)
    out_ref[y] = own[...]
    wait_all(1, NY, across)


def sems(n):
    return pltpu.SemaphoreType.DMA((2, n))


def shape(dims, dtype=F32):
    return jax.ShapeDtypeStruct(dims, dtype)


def call(kernel, ident, inputs, outputs, scratch, name, specs=None, out_specs=None, mib=10):
    params = {"vmem_limit_bytes": mib * 1024 * 1024}
    if ident is None:
        params.update()
    else:
        params.update(collective_id=ident, has_side_effects=True)
    return pl.pallas_call(
        kernel,
        out_shape=outputs,
        in_specs=specs or [VMEM] * len(inputs),
        out_specs=out_specs or [VMEM] * len(outputs),
        scratch_shapes=scratch,
        compiler_params=pltpu.CompilerParams(**params),
        name=name,
    )(*inputs)


PAIR_MIB = 24


def pairs_call(first, lists, geo_s, geo_t, w_s, w_t, cache=None):
    outputs = [shape((16 * NS, 8, 256)), shape((4 * NT, 8, 256))]
    scratch = [pltpu.VMEM((16 * NS + 1, 8, 256), F32), pltpu.VMEM((4 * NT + 1, 8, 256), F32),
               pltpu.VMEM((16 * NS + 1, 8, 256), F32), pltpu.VMEM((4 * NT + 1, 8, 256), F32),
               pltpu.VMEM((2, 32, 128), F32)]
    scratch += [pltpu.VMEM((AT_ONCE, 256, 96), BF16), pltpu.VMEM((AT_ONCE, 3, 96, 256), BF16)]
    if first:
        scratch += [pltpu.VMEM((AT_ONCE, 256, 256), BF16)]
        outputs += [shape((544,), I32), shape((KEPT + 1, AT_ONCE, 256, 256), BF16)]
        acc_s, acc_t, order, cache = call(
            pair_kernel, None, (lists, geo_s, geo_t, w_s, w_t), outputs, scratch, "pairs",
            [SMEM] + [VMEM] * 4, [VMEM, VMEM, SMEM, VMEM], PAIR_MIB,
        )
    else:
        acc_s, acc_t = call(
            again_kernel, None, (lists, geo_s, geo_t, w_s, w_t, cache), outputs, scratch, "again",
            [SMEM] + [VMEM] * 5, None, PAIR_MIB,
        )
        order = lists
    return acc_s.reshape(4 * NS, 32, 256), acc_t.reshape(NT, 32, 256), order, cache


def stay(x):
    return pltpu.with_memory_space_constraint(x, pltpu.HBM)


def shards(positions, facing, area, emission, reflect, pair_list):
    held = stay(pair_list.reshape(128, 2).T)
    emission4, reflect4 = stay(emission.reshape(4, 32, 256)), stay(reflect.reshape(4, 32, 256))
    positions, facing, area, emission = stay(positions), stay(facing), stay(area), stay(emission)
    plane = NX * NY * NC
    geo_s, geo_t, w_s, w_t, lists = call(
        gather_kernel, 0, (positions, facing, area, emission, held),
        [shape((4 * NS, 24, 256)), shape((NT, 24, 256)), shape((4 * NS, 32, 256), BF16),
         shape((NT, 32, 256), BF16), shape((plane, 128), I32)],
        [pltpu.VMEM((3, 16, 256), F32), pltpu.VMEM((2, 16, 256), F32), pltpu.VMEM((16, 256), F32),
         pltpu.VMEM((16, 8, 256), F32), pltpu.VMEM((2, 128), I32), pltpu.SemaphoreType.DMA((5,)),
         pltpu.VMEM((4, 24, 256), F32), pltpu.VMEM((4, 32, 256), BF16), pltpu.VMEM((8, 128), I32),
         pltpu.VMEM((plane, 8, 128), I32), sems(LINE_GATHER), sems(LINE_GATHER), sems(NS), sems(NS), sems(PLANE_GATHER)],
        "gather", [HBM] * 5,
    )

    quarter = pltpu.VMEM((32, 256), F32)
    landing = [pltpu.VMEM((NX, NY, 32, 256), F32), pltpu.VMEM((PLANE, 32, 256), F32),
               pltpu.VMEM((PLANE, 32, 256), F32), pltpu.VMEM((15, 32, 256), F32),
               pltpu.VMEM((4, 32, 256), F32), pltpu.VMEM((4, 32, 256), F32)]
    acc_s, acc_t, order, cache = pairs_call(True, lists, geo_s, geo_t, w_s, w_t)
    w_s, w_t = call(
        turn_kernel, 1, (acc_s, acc_t, emission4, reflect4, area),
        [shape((4 * NS, 32, 256), BF16), shape((NT, 32, 256), BF16)],
        [quarter, quarter, pltpu.VMEM((16, 256), F32), pltpu.SemaphoreType.DMA((3,))]
        + landing + [pltpu.VMEM((32, 256), BF16), sems(NX), sems(PLANE), sems(LINE_SUM),
                   sems(PLANE_GATHER), sems(LINE_GATHER)],
        "turn", [VMEM, VMEM, HBM, HBM, HBM],
    )
    acc_s, acc_t, _, _ = pairs_call(False, order, geo_s, geo_t, w_s, w_t, cache)
    (out,) = call(
        last_kernel, 2, (acc_s, acc_t, emission4, reflect4), [shape((4, 32, 256))],
        [quarter, quarter, pltpu.SemaphoreType.DMA((2,))] + landing + [pltpu.VMEM((32, 256), F32), sems(NX), sems(PLANE), sems(LINE_SUM), sems(NY)],
        "last", [VMEM, VMEM, HBM, HBM],
    )
    return out.reshape(16, 8, 256)


def solution(mesh):
    placed = (
        P(None, "pairs", None),
        P(None, "pairs", None),
        P("pairs", None),
        P("pairs", None, None),
        P("pairs", None, None),
        P("pairs", "rep", None, None, None),
    )
    return jax.shard_map(
        shards, mesh=mesh, in_specs=placed, out_specs=P("pairs", None, None), check_vma=False
    )
```

```python
import functools
import math

import jax
import jax.numpy as jnp
from jax import lax
from jax.experimental import pallas as pl
from jax.experimental.pallas import tpu as pltpu
from jax.sharding import PartitionSpec as P

MESH = pl.DeviceIdType.MESH
VMEM = pl.BlockSpec(memory_space=pltpu.VMEM)
SMEM = pl.BlockSpec(memory_space=pltpu.SMEM)
HBM = pl.BlockSpec(memory_space=pltpu.HBM)
F32, BF16, I32 = jnp.float32, jnp.bfloat16, jnp.int32

NX, NY, NZ, NC = 4, 4, 16, 2
NS, NT = NX * NC, NZ
ROOT_PI = math.sqrt(math.pi)
SOFTEN = 0.1


def place():
    p = lax.axis_index("pairs")
    return p // (NZ * NC), lax.axis_index("rep"), (p // NC) % NZ, p % NC


def device(x, y, z, c):
    return {"pairs": (x * NZ + z) * NC + c, "rep": y}


def plane_peer(me, i):
    x, y, z, c = me
    return (x + i // NY) % NX, (y + i % NY) % NY, z, c


def plane_source(me, i):
    x, y, z, c = me
    return (x - i // NY + NX) % NX, (y - i % NY + NY) % NY, z, c


def sibling(me):
    return me[0], me[1], me[2], 1 - me[3]


def plane_slot(at):
    return (at[0] * NC + at[3]) * NY + at[1]


def line_peer(me, d):
    x, y, z, c = me
    return x, y, (z + d + NZ) % NZ, c


NEAR = (1, -1)
LINE = (1, -1, 2, -2, 3, -3)
LINE_SHORT = LINE + (4, -4)
PLANE = NX * NY


def greet(me, line=LINE):
    barrier = pltpu.get_barrier_semaphore()
    for d in line:
        pl.semaphore_signal(barrier, inc=1, device_id=device(*line_peer(me, d)), device_id_type=MESH)
    pl.semaphore_signal(barrier, inc=1, device_id=device(*sibling(me)), device_id_type=MESH)

    def plane(i, _):
        pl.semaphore_signal(barrier, inc=1, device_id=device(*plane_peer(me, i)), device_id_type=MESH)
        return 0

    lax.fori_loop(1, PLANE, plane, 0)


def met(line=LINE):
    pl.semaphore_wait(pltpu.get_barrier_semaphore(), PLANE + len(line))


def remote(src, dst, sems, i, peer):
    return pltpu.make_async_remote_copy(
        src_ref=src,
        dst_ref=dst,
        send_sem=sems.at[0, i],
        recv_sem=sems.at[1, i],
        device_id=device(*peer),
        device_id_type=MESH,
    )


def start_all(first, last, copy):
    def body(i, _):
        copy(i).start()
        return 0

    lax.fori_loop(first, last, body, 0)


def wait_all(first, last, copy):
    def body(i, _):
        copy(i).wait()
        return 0

    lax.fori_loop(first, last, body, 0)


def line_gather(me, own, into, sems):
    z = me[2]

    def start(source, block, step, n):
        copy = remote(block, into.at[source], sems, n, line_peer(me, step))
        copy.start()
        return copy

    first = [start(z, own, e, n) for n, e in enumerate((3, -3) + NEAR)]
    onward, others = [], []

    def spread(arrived, back, steps, n):
        arrived.wait_recv()
        source = (z + back + NZ) % NZ
        return [start(source, into.at[source], e, n + k) for k, e in enumerate(steps)]

    def from_three():
        for copy, back, n in ((first[0], -3, 4), (first[1], 3, 7)):
            copies = spread(copy, back, (-back,) + NEAR, n)
            onward.append(copies[0])
            others.extend(copies[1:])

    def from_six():
        others.extend(spread(onward[0], -6, NEAR, 10))
        others.extend(spread(onward[1], 6, NEAR + (-2,), 12))

    def end():
        for copy in first[2:] + others:
            copy.wait_recv()
        for copy in first + onward + others:
            copy.wait_send()

    return from_three, from_six, end


LINE_GATHER = 15


def line_gather_short(me, own, into, sems):
    z = me[2]

    def start(source, block, step, n):
        copy = remote(block, into.at[source], sems, n, line_peer(me, step))
        copy.start()
        return copy

    first = [start(z, own, e, n) for n, e in enumerate((4, -4, 3, -3, 2, -2, 1, -1))]
    others = []

    def from_four():
        n = len(first)
        for arrived, back, steps in ((first[0], -4, (4, 3, 2, 1)), (first[1], 4, (-3, -2, -1))):
            arrived.wait_recv()
            source = (z + back + NZ) % NZ
            for e in steps:
                others.append(start(source, into.at[source], e, n))
                n += 1

    def end():
        for copy in first[2:] + others:
            copy.wait_recv()
        for copy in first + others:
            copy.wait_send()

    return from_four, end


def plane_gather(me, own, into, sems):
    def across(i):
        return remote(own, into.at[plane_slot(me)], sems, i, plane_peer(me, i))

    def beside(i):
        block = into.at[plane_slot(plane_source(me, i))]
        return remote(block, block, sems, PLANE + i, sibling(me))

    direct = remote(own, into.at[plane_slot(me)], sems, PLANE, sibling(me))
    start_all(1, PLANE, across)
    direct.start()

    def relay():
        def pass_on(i, _):
            across(i).wait_recv()
            beside(i).start()
            return 0

        lax.fori_loop(1, PLANE, pass_on, 0)

    def end():
        def one(i, _):
            across(i).wait_send()
            beside(i).wait()
            return 0

        lax.fori_loop(1, PLANE, one, 0)
        direct.wait()

    return relay, end


PLANE_GATHER = 2 * PLANE


SLOTS = NS * NY * NT
UNUSED = (16 * NS) | ((4 * NT) << 8)


def pack_entries(me, code, order_ref):
    x, y, z, c = me
    lists = NS * NY
    lane = lax.broadcasted_iota(I32, (lists, 128), 1)
    owner = lax.broadcasted_iota(I32, (lists, 128), 0) >> 2
    code = pltpu.roll(code, (128 - (x * (NZ * NC) + c)) & 127, 1)
    ours = (code >= 0) & (((code >> 2) & 3) == y) & (lane < 2 * NT) & ((lane & 1) == 0)
    entry = (owner * 16 + (code >> 4)) | (((lane >> 1) * 4 + (code & 3)) << 8)
    entry = jnp.where(ours, entry, 0).astype(F32)
    flag = jnp.where(ours, 1.0, 0.0).astype(F32)

    def before(n):
        row, column = (lax.broadcasted_iota(I32, (n, n), k) for k in range(2))
        return row, column

    row, column = before(128)
    inside = jnp.dot(flag.astype(BF16), jnp.where(row < column, 1.0, 0.0).astype(BF16), preferred_element_type=F32)
    row, column = before(lists)
    above = jnp.dot(jnp.where(column < row, 1.0, 0.0).astype(BF16), flag.astype(BF16), preferred_element_type=F32)
    rank = inside + jnp.sum(above, axis=1, keepdims=True)
    rank = jnp.where(ours, rank, -1.0)
    count = jnp.sum(jnp.sum(flag, axis=1, keepdims=True), axis=0, keepdims=True)
    ranks, entries = rank.T, entry.T
    slot = lax.broadcasted_iota(I32, (2 * NT, SLOTS), 1).astype(F32)
    total = jnp.zeros((2 * NT, SLOTS), F32)
    for s in range(lists):
        same = ranks[0 : 2 * NT, s : s + 1] == slot
        total = total + jnp.where(same, entries[0 : 2 * NT, s : s + 1], 0.0)
    total = jnp.sum(total, axis=0, keepdims=True)
    packed = jnp.where(slot[0:1] < count, total, float(UNUSED)).astype(I32)
    order_ref[...] = jnp.full((8, SLOTS + 128), UNUSED, I32)
    order_ref[0:1, 0:SLOTS] = packed
    order_ref[1:2, 0:128] = jnp.broadcast_to(count, (1, 128)).astype(I32)


def gather_kernel(pos_hbm, facing_hbm, area_hbm, emission_hbm, list_hbm,
                  geo_s, geo_t, w_s, w_t, order_ref,
                  pos_ref, facing_ref, area_ref, emission_ref, list_ref, sem_in,
                  own_geo, own_w, own_code, codes, stage, sem_gt, sem_wt, sem_gs, sem_ws, sem_l):
    me = place()
    x, y, z, c = me
    mine = x * NC + c
    greet(me)
    loads = [pltpu.make_async_copy(source, target, sem_in.at[n])
             for n, (source, target) in enumerate(((facing_hbm, facing_ref), (pos_hbm, pos_ref),
                                                   (area_hbm, area_ref), (emission_hbm, emission_ref),
                                                   (list_hbm, list_ref)))]
    for load in loads:
        load.start()
    for load in loads:
        load.wait()
    azimuth, elevation = facing_ref[0], facing_ref[1]
    flat = jnp.cos(elevation)
    parts = [pos_ref[0], pos_ref[1], pos_ref[2],
             jnp.cos(azimuth) * flat, jnp.sin(azimuth) * flat, jnp.sin(elevation)]
    for k in range(4):
        for comp in range(6):
            own_geo[k, comp * 4 : comp * 4 + 4, :] = parts[comp][4 * k : 4 * k + 4, :]
        own_w[k] = jnp.concatenate(
            [area_ref[4 * k + b : 4 * k + b + 1, :] * emission_ref[4 * k + b] for b in range(4)], axis=0
        ).astype(BF16)
    rows, columns = list_ref[0:1, :], list_ref[1:2, :]
    code = jnp.where(rows >= 0, (rows & 15) * 16 + (columns & 15), -1)
    own_code[...] = jnp.broadcast_to(code, (8, 128))
    met()

    def across(own, into, sems, dx):
        return remote(own, into.at[pl.ds(4 * mine, 4)], sems, dx, ((x + dx) % NX, y, z, c))

    def beside(own, into, sems, dx):
        there = pl.ds(4 * (((x - dx + NX) % NX) * NC + c), 4)
        source = own if dx == 0 else into.at[there]
        return remote(source, into.at[there], sems, NX + dx, (x, y, z, 1 - c))

    plane = ((own_geo, geo_s, sem_gs), (own_w, w_s, sem_ws))
    line = (line_gather(me, own_geo.at[y], geo_t, sem_gt), line_gather(me, own_w.at[y], w_t, sem_wt))
    crossing = [across(*args, dx) for args in plane for dx in range(1, NX)]
    siblings = [beside(*args, dx) for args in plane for dx in range(NX)]
    for copy in crossing + [siblings[0], siblings[NX]]:
        copy.start()
    relay_lists, end_lists = plane_gather(me, own_code, codes, sem_l)
    geo_t[z] = own_geo[y]
    w_t[z] = own_w[y]
    geo_s[pl.ds(4 * mine, 4)] = own_geo[...]
    w_s[pl.ds(4 * mine, 4)] = own_w[...]
    codes[mine * NY + y] = own_code[...]
    for n in range(2):
        line[n][0]()
    for n in range(2):
        for dx in range(1, NX):
            crossing[n * (NX - 1) + dx - 1].wait_recv()
            siblings[n * NX + dx].start()
    relay_lists()
    for n in range(2):
        line[n][1]()
    end_lists()
    for s in range(NX * NY * NC):
        stage[s : s + 1, :] = codes[s, 0:1, :]
    pack_entries(me, stage[...], order_ref)
    for copy in crossing:
        copy.wait_send()
    for copy in siblings:
        copy.wait()
    for steps in line:
        steps[2]()


def three(v):
    high = v.astype(BF16)
    rest = v - high.astype(F32)
    middle = rest.astype(BF16)
    return high, middle, (rest - middle.astype(F32)).astype(BF16)


AT_ONCE = 2
KEPT = 128 // AT_ONCE


def unpack_geometry(q, geo, g, spread_geo):
    data = geo[q]
    product = data[0:12] * data[12:24]
    square = data[0:12] * data[0:12]
    product = product[0:4] + product[4:8] + product[8:12]
    square = square[0:4] + square[4:8] + square[8:12]
    for half in range(2):
        lanes = slice(128 * half, 128 * half + 128)
        spread_geo[half, 0:24, :] = data[:, lanes]
        spread_geo[half, 24:28, :] = product[:, lanes]
        spread_geo[half, 28:32, :] = square[:, lanes]
        for b in range(4):
            g[4 * q + b, :, lanes] = spread_geo[half, pl.ds(b, 8, stride=4), :]


def unpack_values(q, w, v):
    values = w[q].astype(F32)
    for b in range(4):
        v[4 * q + b] = values[8 * b : 8 * b + 8]


def clear_tail(*refs):
    for ref in refs:
        ref[ref.shape[0] - 1] = jnp.zeros((8, 256), F32)


def features(entry, g_s, g_t, left, right, k):
    gi, gj = g_s[entry & 255], g_t[entry >> 8]
    row = lax.broadcasted_iota(I32, (8, 256), 0)
    unit = jnp.where(row == 0, 1.0, 0.0).astype(F32)
    zero = jnp.zeros((8, 256), F32)
    h, m, l = three(jnp.concatenate([gi, unit], axis=0))
    left[k] = jnp.concatenate([h, h, m, h, l, m], axis=0).T
    near = jnp.where((row >= 3) & (row < 6), pltpu.roll(gj, 3, 0), jnp.where(row == 6, -1.0, 0.0))
    far = jnp.where(row < 3, pltpu.roll(gj, 5, 0), 0.0)
    far_low = jnp.where(row == 0, -pltpu.roll(gj, 2, 0), 0.0)
    dist = jnp.where(row < 3, (-2.0 * ROOT_PI) * gj, jnp.where(row == 7, ROOT_PI, 0.0))
    dist_low = jnp.where(row == 0, ROOT_PI * (pltpu.roll(gj, 1, 0) + SOFTEN), 0.0)
    for n, (top, low) in enumerate(((near, zero), (far, far_low), (dist, dist_low))):
        h, m, l = three(jnp.concatenate([top, low], axis=0))
        right[k, n] = jnp.concatenate([h, m, h, l, h, m], axis=0)


def couple(left, right, k):
    rows = left[k]
    near, far, dist = [jnp.dot(rows, right[k, n], preferred_element_type=F32) for n in range(3)]
    inverse = pl.reciprocal(dist, approx=False)
    return (jnp.maximum(near, 0.0) * jnp.maximum(far, 0.0) * (inverse * inverse)).astype(BF16)


def apply(entry, kernel, v_s, v_t, acc_s, acc_t):
    i, j = entry & 255, entry >> 8
    acc_s[i & (16 * NS - 1)] += lax.dot_general(
        v_t[j].astype(BF16), kernel, (((1,), (1,)), ((), ())), preferred_element_type=F32
    )
    acc_t[j & (4 * NT - 1)] += jnp.dot(v_s[i].astype(BF16), kernel, preferred_element_type=F32)


def pair_kernel(order, geo_s, geo_t, w_s, w_t, acc_s, acc_t, cache,
                g_s, g_t, v_s, v_t, spread_geo, left, right, held):
    x, y, z, c = place()
    acc_s[...] = jnp.zeros_like(acc_s)
    acc_t[...] = jnp.zeros_like(acc_t)
    clear_tail(g_s, g_t, v_s, v_t)

    def prepare_t(q, _):
        unpack_geometry(q, geo_t, g_t, spread_geo)
        unpack_values(q, w_t, v_t)
        return 0

    def prepare_s(q, _):
        unpack_geometry(q, geo_s, g_s, spread_geo)
        unpack_values(q, w_s, v_s)
        return 0

    lax.fori_loop(0, NT, prepare_t, 0)
    lax.fori_loop(0, 4 * NS, prepare_s, 0)
    turns = (order[1, 0] + AT_ONCE - 1) // AT_ONCE
    held[...] = jnp.zeros_like(held)
    for k in range(AT_ONCE):
        features(order[0, k], g_s, g_t, left, right, k)

    def turn(t, last):
        now = tuple(order[0, AT_ONCE * t + k] for k in range(AT_ONCE))
        kept = jnp.minimum(t, KEPT)
        for k in range(AT_ONCE):
            apply(last[k], held[k], v_s, v_t, acc_s, acc_t)
        for k in range(AT_ONCE):
            kernel = couple(left, right, k)
            held[k] = kernel
            cache[kept, k] = kernel
        for k in range(AT_ONCE):
            features(order[0, AT_ONCE * (t + 1) + k], g_s, g_t, left, right, k)
        return now

    last = lax.fori_loop(0, turns, turn, (jnp.int32(UNUSED),) * AT_ONCE)
    for k in range(AT_ONCE):
        apply(last[k], held[k], v_s, v_t, acc_s, acc_t)


def again_kernel(order, geo_s, geo_t, w_s, w_t, cache, acc_s, acc_t,
                 g_s, g_t, v_s, v_t, spread_geo, left, right):
    turns = (order[1, 0] + AT_ONCE - 1) // AT_ONCE
    acc_s[...] = jnp.zeros_like(acc_s)
    acc_t[...] = jnp.zeros_like(acc_t)
    clear_tail(g_s, g_t, v_s, v_t)

    def prepare_s(q, _):
        unpack_values(q, w_s, v_s)
        return 0

    def prepare_t(q, _):
        unpack_values(q, w_t, v_t)
        return 0

    lax.fori_loop(0, 4 * NS, prepare_s, 0)
    lax.fori_loop(0, NT, prepare_t, 0)

    def turn(t, _):
        for k in range(AT_ONCE):
            apply(order[0, AT_ONCE * t + k], cache[t, k], v_s, v_t, acc_s, acc_t)
        return 0

    lax.fori_loop(0, jnp.minimum(turns, KEPT), turn, 0)

    @pl.when(turns > KEPT)
    def _():
        def shape_s(q, _):
            unpack_geometry(q, geo_s, g_s, spread_geo)
            return 0

        def shape_t(q, _):
            unpack_geometry(q, geo_t, g_t, spread_geo)
            return 0

        def more(t, _):
            entry = order[0, t]
            features(entry, g_s, g_t, left, right, 0)
            apply(entry, couple(left, right, 0), v_s, v_t, acc_s, acc_t)
            return 0

        lax.fori_loop(0, 4 * NS, shape_s, 0)
        lax.fori_loop(0, NT, shape_t, 0)
        lax.fori_loop(AT_ONCE * KEPT, AT_ONCE * turns, more, 0)


def reduce_parts(me, acc_s, acc_t, half_s, sum_s, got_s, got_t, sum_t, far_t, sem_h, sem_s, sem_t):
    x, y, z, c = me

    def halves(n):
        return remote(acc_s.at[pl.ds((n * NC + 1 - c) * NY, NY)], half_s.at[n], sem_h, n, sibling(me))

    def plane(i):
        peer = plane_peer(me, i)
        return remote(sum_s.at[peer[0] * NY + peer[1]], got_s.at[i], sem_s, i, peer)

    def toward(n, h, k, e):
        piece = acc_t.at[(z + e - h + NZ) % NZ]
        return remote(piece, got_t.at[3 * n + k], sem_t, 3 * n + k, line_peer(me, e))

    start_all(0, NX, halves)
    hubs = (6, -6, 3, -3, 0)
    near = [[toward(n, h, k, e) for k, e in enumerate(NEAR + (2,) if h == -6 else NEAR)]
            for n, h in enumerate(hubs)]
    for copies in near:
        for copy in copies:
            copy.start()
    for n in range(NX):
        halves(n).wait_recv()
        sum_s[n * NY : n * NY + NY] = acc_s[pl.ds((n * NC + c) * NY, NY)] + half_s[n]
    start_all(1, PLANE, plane)
    far = []
    for n, h in enumerate(hubs):
        part = acc_t[(z - h + NZ) % NZ]
        for k, copy in enumerate(near[n]):
            copy.wait_recv()
            part = part + got_t[3 * n + k]
        if abs(h) == 3:
            far[n - 2].wait_recv()
            part = part + far_t[n - 2]
        if h:
            sum_t[n] = part
            far.append(remote(sum_t.at[n], far_t.at[n], sem_t, 15 + n, line_peer(me, -3 if h > 0 else 3)))
            far[n].start()
    total = part + sum_s[x * NY + y]
    wait_all(1, PLANE, plane)
    total = lax.fori_loop(1, PLANE, lambda i, t: t + got_s[i], total)
    for n in (2, 3):
        far[n].wait_recv()
        total = total + far_t[n]
    for n in range(NX):
        halves(n).wait_send()
    for copies in near:
        for copy in copies:
            copy.wait_send()
    for copy in far:
        copy.wait_send()
    return total


LINE_SUM = 19


def turn_kernel(acc_s, acc_t, emission_hbm, reflect_hbm, area_hbm, w_s, w_t,
                emission_ref, reflect_ref, area_ref, sem_in,
                half_s, sum_s, got_s, got_t, sum_t, far_t, own_w,
                sem_h, sem_s, sem_t, sem_ws, sem_wt):
    me = place()
    x, y, z, c = me
    greet(me, LINE_SHORT)
    loads = [pltpu.make_async_copy(source, target, sem_in.at[n])
             for n, (source, target) in enumerate(((emission_hbm.at[y], emission_ref),
                                                   (reflect_hbm.at[y], reflect_ref), (area_hbm, area_ref)))]
    for load in loads:
        load.start()
    met(LINE_SHORT)
    total = reduce_parts(
        me, acc_s, acc_t, half_s, sum_s, got_s, got_t, sum_t, far_t, sem_h, sem_s, sem_t
    )
    for load in loads:
        load.wait()
    radiosity = emission_ref[...] + reflect_ref[...] * total
    area = jnp.concatenate(
        [jnp.broadcast_to(area_ref[pl.ds(4 * y + b, 1), :], (8, 256)) for b in range(4)], axis=0
    )
    own_w[...] = (area * radiosity).astype(BF16)
    from_four, end_line = line_gather_short(me, own_w, w_t, sem_wt)
    relay, end_plane = plane_gather(me, own_w, w_s, sem_ws)
    w_t[z] = own_w[...]
    w_s[plane_slot(me)] = own_w[...]
    relay()
    from_four()
    end_plane()
    end_line()


def last_kernel(acc_s, acc_t, emission_hbm, reflect_hbm, out_ref,
                emission_ref, reflect_ref, sem_in,
                half_s, sum_s, got_s, got_t, sum_t, far_t, own,
                sem_h, sem_s, sem_t, sem_o):
    me = place()
    x, y, z, c = me
    greet(me)
    loads = [pltpu.make_async_copy(source, target, sem_in.at[n])
             for n, (source, target) in enumerate(((emission_hbm.at[y], emission_ref),
                                                   (reflect_hbm.at[y], reflect_ref)))]
    for load in loads:
        load.start()
    met()
    total = reduce_parts(
        me, acc_s, acc_t, half_s, sum_s, got_s, got_t, sum_t, far_t, sem_h, sem_s, sem_t
    )
    for load in loads:
        load.wait()
    own[...] = emission_ref[...] + reflect_ref[...] * total

    def across(i):
        return remote(own, out_ref.at[y], sem_o, i, (x, (y + i) % NY, z, c))

    start_all(1, NY, across)
    out_ref[y] = own[...]
    wait_all(1, NY, across)


def sems(n):
    return pltpu.SemaphoreType.DMA((2, n))


def shape(dims, dtype=F32):
    return jax.ShapeDtypeStruct(dims, dtype)


def call(kernel, ident, inputs, outputs, scratch, name, specs=None, out_specs=None, mib=10):
    params = {"vmem_limit_bytes": mib * 1024 * 1024}
    if ident is None:
        params.update()
    else:
        params.update(collective_id=ident, has_side_effects=True)
    return pl.pallas_call(
        kernel,
        out_shape=outputs,
        in_specs=specs or [VMEM] * len(inputs),
        out_specs=out_specs or [VMEM] * len(outputs),
        scratch_shapes=scratch,
        compiler_params=pltpu.CompilerParams(**params),
        name=name,
    )(*inputs)


PAIR_MIB = 24


def pairs_call(first, lists, geo_s, geo_t, w_s, w_t, cache=None):
    outputs = [shape((16 * NS, 8, 256)), shape((4 * NT, 8, 256))]
    scratch = [pltpu.VMEM((16 * NS + 1, 8, 256), F32), pltpu.VMEM((4 * NT + 1, 8, 256), F32),
               pltpu.VMEM((16 * NS + 1, 8, 256), F32), pltpu.VMEM((4 * NT + 1, 8, 256), F32),
               pltpu.VMEM((2, 32, 128), F32)]
    scratch += [pltpu.VMEM((AT_ONCE, 256, 96), BF16), pltpu.VMEM((AT_ONCE, 3, 96, 256), BF16)]
    if first:
        scratch += [pltpu.VMEM((AT_ONCE, 256, 256), BF16)]
        outputs += [shape((KEPT + 1, AT_ONCE, 256, 256), BF16)]
        acc_s, acc_t, cache = call(
            pair_kernel, None, (lists, geo_s, geo_t, w_s, w_t), outputs, scratch, "pairs",
            [SMEM] + [VMEM] * 4, [VMEM, VMEM, VMEM], PAIR_MIB,
        )
    else:
        acc_s, acc_t = call(
            again_kernel, None, (lists, geo_s, geo_t, w_s, w_t, cache), outputs, scratch, "again",
            [SMEM] + [VMEM] * 5, None, PAIR_MIB,
        )
    return acc_s.reshape(4 * NS, 32, 256), acc_t.reshape(NT, 32, 256), cache


def stay(x):
    return pltpu.with_memory_space_constraint(x, pltpu.HBM)


def shards(positions, facing, area, emission, reflect, pair_list):
    held = stay(pair_list.reshape(128, 2).T)
    emission4, reflect4 = stay(emission.reshape(4, 32, 256)), stay(reflect.reshape(4, 32, 256))
    positions, facing, area, emission = stay(positions), stay(facing), stay(area), stay(emission)
    plane = NX * NY * NC
    geo_s, geo_t, w_s, w_t, order = call(
        gather_kernel, 0, (positions, facing, area, emission, held),
        [shape((4 * NS, 24, 256)), shape((NT, 24, 256)), shape((4 * NS, 32, 256), BF16),
         shape((NT, 32, 256), BF16), shape((8, SLOTS + 128), I32)],
        [pltpu.VMEM((3, 16, 256), F32), pltpu.VMEM((2, 16, 256), F32), pltpu.VMEM((16, 256), F32),
         pltpu.VMEM((16, 8, 256), F32), pltpu.VMEM((2, 128), I32), pltpu.SemaphoreType.DMA((5,)),
         pltpu.VMEM((4, 24, 256), F32), pltpu.VMEM((4, 32, 256), BF16), pltpu.VMEM((8, 128), I32),
         pltpu.VMEM((plane, 8, 128), I32), pltpu.VMEM((plane, 128), I32), sems(LINE_GATHER), sems(LINE_GATHER), sems(NS), sems(NS), sems(PLANE_GATHER)],
        "gather", [HBM] * 5,
    )

    quarter = pltpu.VMEM((32, 256), F32)
    landing = [pltpu.VMEM((NX, NY, 32, 256), F32), pltpu.VMEM((PLANE, 32, 256), F32),
               pltpu.VMEM((PLANE, 32, 256), F32), pltpu.VMEM((15, 32, 256), F32),
               pltpu.VMEM((4, 32, 256), F32), pltpu.VMEM((4, 32, 256), F32)]
    acc_s, acc_t, cache = pairs_call(True, order, geo_s, geo_t, w_s, w_t)
    w_s, w_t = call(
        turn_kernel, 1, (acc_s, acc_t, emission4, reflect4, area),
        [shape((4 * NS, 32, 256), BF16), shape((NT, 32, 256), BF16)],
        [quarter, quarter, pltpu.VMEM((16, 256), F32), pltpu.SemaphoreType.DMA((3,))]
        + landing + [pltpu.VMEM((32, 256), BF16), sems(NX), sems(PLANE), sems(LINE_SUM),
                   sems(PLANE_GATHER), sems(LINE_GATHER)],
        "turn", [VMEM, VMEM, HBM, HBM, HBM],
    )
    acc_s, acc_t, _ = pairs_call(False, order, geo_s, geo_t, w_s, w_t, cache)
    (out,) = call(
        last_kernel, 2, (acc_s, acc_t, emission4, reflect4), [shape((4, 32, 256))],
        [quarter, quarter, pltpu.SemaphoreType.DMA((2,))] + landing + [pltpu.VMEM((32, 256), F32), sems(NX), sems(PLANE), sems(LINE_SUM), sems(NY)],
        "last", [VMEM, VMEM, HBM, HBM],
    )
    return out.reshape(16, 8, 256)


def solution(mesh):
    placed = (
        P(None, "pairs", None),
        P(None, "pairs", None),
        P("pairs", None),
        P("pairs", None, None),
        P("pairs", None, None),
        P("pairs", "rep", None, None, None),
    )
    return jax.shard_map(
        shards, mesh=mesh, in_specs=placed, out_specs=P("pairs", None, None), check_vma=False
    )
```

```python
import functools
import math

import jax
import jax.numpy as jnp
from jax import lax
from jax.experimental import pallas as pl
from jax.experimental.pallas import tpu as pltpu
from jax.sharding import PartitionSpec as P

MESH = pl.DeviceIdType.MESH
VMEM = pl.BlockSpec(memory_space=pltpu.VMEM)
SMEM = pl.BlockSpec(memory_space=pltpu.SMEM)
HBM = pl.BlockSpec(memory_space=pltpu.HBM)
F32, BF16, I32 = jnp.float32, jnp.bfloat16, jnp.int32

NX, NY, NZ, NC = 4, 4, 16, 2
NS, NT = NX * NC, NZ
ROOT_PI = math.sqrt(math.pi)
SOFTEN = 0.1


def place():
    p = lax.axis_index("pairs")
    return p // (NZ * NC), lax.axis_index("rep"), (p // NC) % NZ, p % NC


def device(x, y, z, c):
    return {"pairs": (x * NZ + z) * NC + c, "rep": y}


def plane_peer(me, i):
    x, y, z, c = me
    return (x + i // NY) % NX, (y + i % NY) % NY, z, c


def plane_source(me, i):
    x, y, z, c = me
    return (x - i // NY + NX) % NX, (y - i % NY + NY) % NY, z, c


def sibling(me):
    return me[0], me[1], me[2], 1 - me[3]


def plane_slot(at):
    return (at[0] * NC + at[3]) * NY + at[1]


def line_peer(me, d):
    x, y, z, c = me
    return x, y, (z + d + NZ) % NZ, c


NEAR = (1, -1)
LINE = (1, -1, 2, -2, 3, -3)
LINE_SHORT = LINE + (4, -4)
PLANE = NX * NY


def greet(me, line=LINE):
    barrier = pltpu.get_barrier_semaphore()
    for d in line:
        pl.semaphore_signal(barrier, inc=1, device_id=device(*line_peer(me, d)), device_id_type=MESH)
    pl.semaphore_signal(barrier, inc=1, device_id=device(*sibling(me)), device_id_type=MESH)

    def plane(i, _):
        pl.semaphore_signal(barrier, inc=1, device_id=device(*plane_peer(me, i)), device_id_type=MESH)
        return 0

    lax.fori_loop(1, PLANE, plane, 0)


def met(line=LINE):
    pl.semaphore_wait(pltpu.get_barrier_semaphore(), PLANE + len(line))


def remote(src, dst, sems, i, peer):
    return pltpu.make_async_remote_copy(
        src_ref=src,
        dst_ref=dst,
        send_sem=sems.at[0, i],
        recv_sem=sems.at[1, i],
        device_id=device(*peer),
        device_id_type=MESH,
    )


def start_all(first, last, copy):
    def body(i, _):
        copy(i).start()
        return 0

    lax.fori_loop(first, last, body, 0)


def wait_all(first, last, copy):
    def body(i, _):
        copy(i).wait()
        return 0

    lax.fori_loop(first, last, body, 0)


def line_gather(me, own, into, sems):
    z = me[2]

    def start(source, block, step, n):
        copy = remote(block, into.at[source], sems, n, line_peer(me, step))
        copy.start()
        return copy

    first = [start(z, own, e, n) for n, e in enumerate((3, -3) + NEAR)]
    onward, others = [], []

    def spread(arrived, back, steps, n):
        arrived.wait_recv()
        source = (z + back + NZ) % NZ
        return [start(source, into.at[source], e, n + k) for k, e in enumerate(steps)]

    def from_three():
        for copy, back, n in ((first[0], -3, 4), (first[1], 3, 7)):
            copies = spread(copy, back, (-back,) + NEAR, n)
            onward.append(copies[0])
            others.extend(copies[1:])

    def from_six():
        others.extend(spread(onward[0], -6, NEAR, 10))
        others.extend(spread(onward[1], 6, NEAR + (-2,), 12))

    def end():
        for copy in first[2:] + others:
            copy.wait_recv()
        for copy in first + onward + others:
            copy.wait_send()

    return from_three, from_six, end


LINE_GATHER = 15


def line_gather_short(me, own, into, sems):
    z = me[2]

    def start(source, block, step, n):
        copy = remote(block, into.at[source], sems, n, line_peer(me, step))
        copy.start()
        return copy

    first = [start(z, own, e, n) for n, e in enumerate((4, -4, 3, -3, 2, -2, 1, -1))]
    others = []

    def from_four():
        n = len(first)
        for arrived, back, steps in ((first[0], -4, (4, 3, 2, 1)), (first[1], 4, (-3, -2, -1))):
            arrived.wait_recv()
            source = (z + back + NZ) % NZ
            for e in steps:
                others.append(start(source, into.at[source], e, n))
                n += 1

    def end():
        for copy in first[2:] + others:
            copy.wait_recv()
        for copy in first + others:
            copy.wait_send()

    return from_four, end


def plane_gather(me, own, into, sems):
    def across(i):
        return remote(own, into.at[plane_slot(me)], sems, i, plane_peer(me, i))

    def beside(i):
        block = into.at[plane_slot(plane_source(me, i))]
        return remote(block, block, sems, PLANE + i, sibling(me))

    direct = remote(own, into.at[plane_slot(me)], sems, PLANE, sibling(me))
    start_all(1, PLANE, across)
    direct.start()

    def relay():
        def pass_on(i, _):
            across(i).wait_recv()
            beside(i).start()
            return 0

        lax.fori_loop(1, PLANE, pass_on, 0)

    def end():
        def one(i, _):
            across(i).wait_send()
            beside(i).wait()
            return 0

        lax.fori_loop(1, PLANE, one, 0)
        direct.wait()

    return relay, end


PLANE_GATHER = 2 * PLANE


SLOTS = NS * NY * NT
UNUSED = (16 * NS) | ((4 * NT) << 8)


def pack_entries(me, code, order_ref):
    x, y, z, c = me
    lists = NS * NY
    lane = lax.broadcasted_iota(I32, (lists, 128), 1)
    owner = lax.broadcasted_iota(I32, (lists, 128), 0) >> 2
    code = pltpu.roll(code, (128 - (x * (NZ * NC) + c)) & 127, 1)
    ours = (code >= 0) & (((code >> 2) & 3) == y) & (lane < 2 * NT) & ((lane & 1) == 0)
    entry = (owner * 16 + (code >> 4)) | (((lane >> 1) * 4 + (code & 3)) << 8)
    entry = jnp.where(ours, entry, 0).astype(F32)
    flag = jnp.where(ours, 1.0, 0.0).astype(F32)

    def before(n):
        row, column = (lax.broadcasted_iota(I32, (n, n), k) for k in range(2))
        return row, column

    row, column = before(128)
    inside = jnp.dot(flag.astype(BF16), jnp.where(row < column, 1.0, 0.0).astype(BF16), preferred_element_type=F32)
    row, column = before(lists)
    above = jnp.dot(jnp.where(column < row, 1.0, 0.0).astype(BF16), flag.astype(BF16), preferred_element_type=F32)
    rank = inside + jnp.sum(above, axis=1, keepdims=True)
    rank = jnp.where(ours, rank, -1.0)
    count = jnp.sum(jnp.sum(flag, axis=1, keepdims=True), axis=0, keepdims=True)
    ranks, entries = rank.T, entry.T
    slot = lax.broadcasted_iota(I32, (2 * NT, SLOTS), 1).astype(F32)
    total = jnp.zeros((2 * NT, SLOTS), F32)
    for s in range(lists):
        same = ranks[0 : 2 * NT, s : s + 1] == slot
        total = total + jnp.where(same, entries[0 : 2 * NT, s : s + 1], 0.0)
    total = jnp.sum(total, axis=0, keepdims=True)
    packed = jnp.where(slot[0:1] < count, total, float(UNUSED)).astype(I32)
    order_ref[...] = jnp.full((8, SLOTS + 128), UNUSED, I32)
    order_ref[0:1, 0:SLOTS] = packed
    order_ref[1:2, 0:128] = jnp.broadcast_to(count, (1, 128)).astype(I32)


def gather_kernel(pos_hbm, facing_hbm, area_hbm, emission_hbm, list_hbm,
                  geo_s, geo_t, w_s, w_t, order_ref,
                  pos_ref, facing_ref, area_ref, emission_ref, list_ref, sem_in,
                  own_geo, own_w, own_code, codes, stage, sem_gt, sem_wt, sem_gs, sem_ws, sem_l):
    me = place()
    x, y, z, c = me
    mine = x * NC + c
    greet(me)
    loads = [pltpu.make_async_copy(source, target, sem_in.at[n])
             for n, (source, target) in enumerate(((facing_hbm, facing_ref), (pos_hbm, pos_ref),
                                                   (area_hbm, area_ref), (emission_hbm, emission_ref),
                                                   (list_hbm, list_ref)))]
    for load in loads:
        load.start()
    for load in loads:
        load.wait()
    azimuth, elevation = facing_ref[0], facing_ref[1]
    flat = jnp.cos(elevation)
    parts = [pos_ref[0], pos_ref[1], pos_ref[2],
             jnp.cos(azimuth) * flat, jnp.sin(azimuth) * flat, jnp.sin(elevation)]
    for k in range(4):
        for comp in range(6):
            own_geo[k, comp * 4 : comp * 4 + 4, :] = parts[comp][4 * k : 4 * k + 4, :]
        own_w[k] = jnp.concatenate(
            [area_ref[4 * k + b : 4 * k + b + 1, :] * emission_ref[4 * k + b] for b in range(4)], axis=0
        ).astype(BF16)
    rows, columns = list_ref[0:1, :], list_ref[1:2, :]
    code = jnp.where(rows >= 0, (rows & 15) * 16 + (columns & 15), -1)
    own_code[...] = jnp.broadcast_to(code, (8, 128))
    met()

    def across(own, into, sems, dx):
        return remote(own, into.at[pl.ds(4 * mine, 4)], sems, dx, ((x + dx) % NX, y, z, c))

    def beside(own, into, sems, dx):
        there = pl.ds(4 * (((x - dx + NX) % NX) * NC + c), 4)
        source = own if dx == 0 else into.at[there]
        return remote(source, into.at[there], sems, NX + dx, (x, y, z, 1 - c))

    plane = ((own_geo, geo_s, sem_gs), (own_w, w_s, sem_ws))
    line = (line_gather(me, own_geo.at[y], geo_t, sem_gt), line_gather(me, own_w.at[y], w_t, sem_wt))
    crossing = [across(*args, dx) for args in plane for dx in range(1, NX)]
    siblings = [beside(*args, dx) for args in plane for dx in range(NX)]
    for copy in crossing + [siblings[0], siblings[NX]]:
        copy.start()
    relay_lists, end_lists = plane_gather(me, own_code, codes, sem_l)
    geo_t[z] = own_geo[y]
    w_t[z] = own_w[y]
    geo_s[pl.ds(4 * mine, 4)] = own_geo[...]
    w_s[pl.ds(4 * mine, 4)] = own_w[...]
    codes[mine * NY + y] = own_code[...]
    for n in range(2):
        line[n][0]()
    for n in range(2):
        for dx in range(1, NX):
            crossing[n * (NX - 1) + dx - 1].wait_recv()
            siblings[n * NX + dx].start()
    relay_lists()
    for n in range(2):
        line[n][1]()
    end_lists()
    for s in range(NX * NY * NC):
        stage[s : s + 1, :] = codes[s, 0:1, :]
    pack_entries(me, stage[...], order_ref)
    for copy in crossing:
        copy.wait_send()
    for copy in siblings:
        copy.wait()
    for steps in line:
        steps[2]()


def three(v):
    high = v.astype(BF16)
    rest = v - high.astype(F32)
    middle = rest.astype(BF16)
    return high, middle, (rest - middle.astype(F32)).astype(BF16)


AT_ONCE = 2
KEPT = 128 // AT_ONCE


def unpack_geometry(q, geo, g, spread_geo):
    data = geo[q]
    product = data[0:12] * data[12:24]
    square = data[0:12] * data[0:12]
    product = product[0:4] + product[4:8] + product[8:12]
    square = square[0:4] + square[4:8] + square[8:12]
    for half in range(2):
        lanes = slice(128 * half, 128 * half + 128)
        spread_geo[half, 0:24, :] = data[:, lanes]
        spread_geo[half, 24:28, :] = product[:, lanes]
        spread_geo[half, 28:32, :] = square[:, lanes]
        for b in range(4):
            g[4 * q + b, :, lanes] = spread_geo[half, pl.ds(b, 8, stride=4), :]


def unpack_values(q, w, v):
    values = w[q].astype(F32)
    for b in range(4):
        v[4 * q + b] = values[8 * b : 8 * b + 8]


def clear_tail(*refs):
    for ref in refs:
        ref[ref.shape[0] - 1] = jnp.zeros((8, 256), F32)


def features(entry, g_s, g_t, left, right, k):
    gi, gj = g_s[entry & 255], g_t[entry >> 8]
    row = lax.broadcasted_iota(I32, (8, 256), 0)
    unit = jnp.where(row == 0, 1.0, 0.0).astype(F32)
    zero = jnp.zeros((8, 256), F32)
    h, m, l = three(jnp.concatenate([gi, unit], axis=0))
    left[k] = jnp.concatenate([h, h, m, h, l, m], axis=0).T
    near = jnp.where((row >= 3) & (row < 6), pltpu.roll(gj, 3, 0), jnp.where(row == 6, -1.0, 0.0))
    far = jnp.where(row < 3, pltpu.roll(gj, 5, 0), 0.0)
    far_low = jnp.where(row == 0, -pltpu.roll(gj, 2, 0), 0.0)
    dist = jnp.where(row < 3, (-2.0 * ROOT_PI) * gj, jnp.where(row == 7, ROOT_PI, 0.0))
    dist_low = jnp.where(row == 0, ROOT_PI * (pltpu.roll(gj, 1, 0) + SOFTEN), 0.0)
    for n, (top, low) in enumerate(((near, zero), (far, far_low), (dist, dist_low))):
        h, m, l = three(jnp.concatenate([top, low], axis=0))
        right[k, n] = jnp.concatenate([h, m, h, l, h, m], axis=0)


def couple(left, right, k):
    rows = left[k]
    near, far, dist = [jnp.dot(rows, right[k, n], preferred_element_type=F32) for n in range(3)]
    inverse = pl.reciprocal(dist, approx=False)
    return (jnp.maximum(near, 0.0) * jnp.maximum(far, 0.0) * (inverse * inverse)).astype(BF16)


def apply(entry, kernel, v_s, v_t, acc_s, acc_t):
    i, j = entry & 255, entry >> 8
    acc_s[i & (16 * NS - 1)] += lax.dot_general(
        v_t[j].astype(BF16), kernel, (((1,), (1,)), ((), ())), preferred_element_type=F32
    )
    acc_t[j & (4 * NT - 1)] += jnp.dot(v_s[i].astype(BF16), kernel, preferred_element_type=F32)


def pair_kernel(order, geo_s, geo_t, w_s, w_t, acc_s, acc_t, cache,
                g_s, g_t, v_s, v_t, spread_geo, left, right, held):
    x, y, z, c = place()
    acc_s[...] = jnp.zeros_like(acc_s)
    acc_t[...] = jnp.zeros_like(acc_t)
    clear_tail(g_s, g_t, v_s, v_t)

    def prepare_t(q, _):
        unpack_geometry(q, geo_t, g_t, spread_geo)
        unpack_values(q, w_t, v_t)
        return 0

    def prepare_s(q, _):
        unpack_geometry(q, geo_s, g_s, spread_geo)
        unpack_values(q, w_s, v_s)
        return 0

    lax.fori_loop(0, NT, prepare_t, 0)
    lax.fori_loop(0, 4 * NS, prepare_s, 0)
    turns = (order[1, 0] + AT_ONCE - 1) // AT_ONCE
    held[...] = jnp.zeros_like(held)
    for k in range(AT_ONCE):
        features(order[0, k], g_s, g_t, left, right, k)

    def turn(t, last):
        now = tuple(order[0, AT_ONCE * t + k] for k in range(AT_ONCE))
        kept = jnp.minimum(t, KEPT)
        for k in range(AT_ONCE):
            apply(last[k], held[k], v_s, v_t, acc_s, acc_t)
        for k in range(AT_ONCE):
            kernel = couple(left, right, k)
            held[k] = kernel
            cache[kept, k] = kernel
        for k in range(AT_ONCE):
            features(order[0, AT_ONCE * (t + 1) + k], g_s, g_t, left, right, k)
        return now

    last = lax.fori_loop(0, turns, turn, (jnp.int32(UNUSED),) * AT_ONCE)
    for k in range(AT_ONCE):
        apply(last[k], held[k], v_s, v_t, acc_s, acc_t)


def again_kernel(order, geo_s, geo_t, w_s, w_t, cache, acc_s, acc_t,
                 g_s, g_t, v_s, v_t, spread_geo, left, right):
    turns = (order[1, 0] + AT_ONCE - 1) // AT_ONCE
    acc_s[...] = jnp.zeros_like(acc_s)
    acc_t[...] = jnp.zeros_like(acc_t)
    clear_tail(g_s, g_t, v_s, v_t)

    def prepare_s(q, _):
        unpack_values(q, w_s, v_s)
        return 0

    def prepare_t(q, _):
        unpack_values(q, w_t, v_t)
        return 0

    lax.fori_loop(0, 4 * NS, prepare_s, 0)
    lax.fori_loop(0, NT, prepare_t, 0)

    def turn(t, _):
        for k in range(AT_ONCE):
            apply(order[0, AT_ONCE * t + k], cache[t, k], v_s, v_t, acc_s, acc_t)
        return 0

    lax.fori_loop(0, jnp.minimum(turns, KEPT), turn, 0)

    @pl.when(turns > KEPT)
    def _():
        def shape_s(q, _):
            unpack_geometry(q, geo_s, g_s, spread_geo)
            return 0

        def shape_t(q, _):
            unpack_geometry(q, geo_t, g_t, spread_geo)
            return 0

        def more(t, _):
            entry = order[0, t]
            features(entry, g_s, g_t, left, right, 0)
            apply(entry, couple(left, right, 0), v_s, v_t, acc_s, acc_t)
            return 0

        lax.fori_loop(0, 4 * NS, shape_s, 0)
        lax.fori_loop(0, NT, shape_t, 0)
        lax.fori_loop(AT_ONCE * KEPT, AT_ONCE * turns, more, 0)


def reduce_parts(me, acc_s, acc_t, half_s, sum_s, got_s, got_t, sum_t, far_t, sem_h, sem_s, sem_t):
    x, y, z, c = me

    def halves(dx):
        n = (x + dx) % NX
        return remote(acc_s.at[pl.ds((n * NC + 1 - c) * NY, NY)], half_s.at[dx], sem_h, dx, sibling(me))

    def plane(i):
        peer = plane_peer(me, i)
        return remote(sum_s.at[peer[0] * NY + peer[1]], got_s.at[i], sem_s, i, peer)

    def toward(n, h, k, e):
        piece = acc_t.at[(z + e - h + NZ) % NZ]
        return remote(piece, got_t.at[3 * n + k], sem_t, 3 * n + k, line_peer(me, e))

    for dx in (2, 1, 3, 0):
        halves(dx).start()
    hubs = (6, -6, 3, -3, 0)
    near = [[toward(n, h, k, e) for k, e in enumerate(NEAR + (2,) if h == -6 else NEAR)]
            for n, h in enumerate(hubs)]
    for copies in near:
        for copy in copies:
            copy.start()
    for dx in (2, 1, 3, 0):
        halves(dx).wait_recv()
        n = (x + dx) % NX
        sum_s[pl.ds(n * NY, NY)] = acc_s[pl.ds((n * NC + c) * NY, NY)] + half_s[dx]
        start_all(max(1, dx * NY), dx * NY + NY, plane)
    far = []
    for n, h in enumerate(hubs):
        part = acc_t[(z - h + NZ) % NZ]
        for k, copy in enumerate(near[n]):
            copy.wait_recv()
            part = part + got_t[3 * n + k]
        if abs(h) == 3:
            far[n - 2].wait_recv()
            part = part + far_t[n - 2]
        if h:
            sum_t[n] = part
            far.append(remote(sum_t.at[n], far_t.at[n], sem_t, 15 + n, line_peer(me, -3 if h > 0 else 3)))
            far[n].start()
    total = part + sum_s[x * NY + y]
    wait_all(1, PLANE, plane)
    total = lax.fori_loop(1, PLANE, lambda i, t: t + got_s[i], total)
    for n in (2, 3):
        far[n].wait_recv()
        total = total + far_t[n]
    for n in range(NX):
        halves(n).wait_send()
    for copies in near:
        for copy in copies:
            copy.wait_send()
    for copy in far:
        copy.wait_send()
    return total


LINE_SUM = 19


def turn_kernel(acc_s, acc_t, emission_hbm, reflect_hbm, area_hbm, w_s, w_t,
                emission_ref, reflect_ref, area_ref, sem_in,
                half_s, sum_s, got_s, got_t, sum_t, far_t, own_w,
                sem_h, sem_s, sem_t, sem_ws, sem_wt):
    me = place()
    x, y, z, c = me
    greet(me, LINE_SHORT)
    loads = [pltpu.make_async_copy(source, target, sem_in.at[n])
             for n, (source, target) in enumerate(((emission_hbm.at[y], emission_ref),
                                                   (reflect_hbm.at[y], reflect_ref), (area_hbm, area_ref)))]
    for load in loads:
        load.start()
    met(LINE_SHORT)
    total = reduce_parts(
        me, acc_s, acc_t, half_s, sum_s, got_s, got_t, sum_t, far_t, sem_h, sem_s, sem_t
    )
    for load in loads:
        load.wait()
    radiosity = emission_ref[...] + reflect_ref[...] * total
    area = jnp.concatenate(
        [jnp.broadcast_to(area_ref[pl.ds(4 * y + b, 1), :], (8, 256)) for b in range(4)], axis=0
    )
    own_w[...] = (area * radiosity).astype(BF16)
    from_four, end_line = line_gather_short(me, own_w, w_t, sem_wt)
    relay, end_plane = plane_gather(me, own_w, w_s, sem_ws)
    w_t[z] = own_w[...]
    w_s[plane_slot(me)] = own_w[...]
    relay()
    from_four()
    end_plane()
    end_line()


def last_kernel(acc_s, acc_t, emission_hbm, reflect_hbm, out_ref,
                emission_ref, reflect_ref, sem_in,
                half_s, sum_s, got_s, got_t, sum_t, far_t, own,
                sem_h, sem_s, sem_t, sem_o):
    me = place()
    x, y, z, c = me
    greet(me)
    loads = [pltpu.make_async_copy(source, target, sem_in.at[n])
             for n, (source, target) in enumerate(((emission_hbm.at[y], emission_ref),
                                                   (reflect_hbm.at[y], reflect_ref)))]
    for load in loads:
        load.start()
    met()
    total = reduce_parts(
        me, acc_s, acc_t, half_s, sum_s, got_s, got_t, sum_t, far_t, sem_h, sem_s, sem_t
    )
    for load in loads:
        load.wait()
    own[...] = emission_ref[...] + reflect_ref[...] * total

    def across(i):
        return remote(own, out_ref.at[y], sem_o, i, (x, (y + i) % NY, z, c))

    start_all(1, NY, across)
    out_ref[y] = own[...]
    wait_all(1, NY, across)


def sems(n):
    return pltpu.SemaphoreType.DMA((2, n))


def shape(dims, dtype=F32):
    return jax.ShapeDtypeStruct(dims, dtype)


def call(kernel, ident, inputs, outputs, scratch, name, specs=None, out_specs=None, mib=10):
    params = {"vmem_limit_bytes": mib * 1024 * 1024}
    if ident is None:
        params.update()
    else:
        params.update(collective_id=ident, has_side_effects=True)
    return pl.pallas_call(
        kernel,
        out_shape=outputs,
        in_specs=specs or [VMEM] * len(inputs),
        out_specs=out_specs or [VMEM] * len(outputs),
        scratch_shapes=scratch,
        compiler_params=pltpu.CompilerParams(**params),
        name=name,
    )(*inputs)


PAIR_MIB = 24


def pairs_call(first, lists, geo_s, geo_t, w_s, w_t, cache=None):
    outputs = [shape((16 * NS, 8, 256)), shape((4 * NT, 8, 256))]
    scratch = [pltpu.VMEM((16 * NS + 1, 8, 256), F32), pltpu.VMEM((4 * NT + 1, 8, 256), F32),
               pltpu.VMEM((16 * NS + 1, 8, 256), F32), pltpu.VMEM((4 * NT + 1, 8, 256), F32),
               pltpu.VMEM((2, 32, 128), F32)]
    scratch += [pltpu.VMEM((AT_ONCE, 256, 96), BF16), pltpu.VMEM((AT_ONCE, 3, 96, 256), BF16)]
    if first:
        scratch += [pltpu.VMEM((AT_ONCE, 256, 256), BF16)]
        outputs += [shape((KEPT + 1, AT_ONCE, 256, 256), BF16)]
        acc_s, acc_t, cache = call(
            pair_kernel, None, (lists, geo_s, geo_t, w_s, w_t), outputs, scratch, "pairs",
            [SMEM] + [VMEM] * 4, [VMEM, VMEM, VMEM], PAIR_MIB,
        )
    else:
        acc_s, acc_t = call(
            again_kernel, None, (lists, geo_s, geo_t, w_s, w_t, cache), outputs, scratch, "again",
            [SMEM] + [VMEM] * 5, None, PAIR_MIB,
        )
    return acc_s.reshape(4 * NS, 32, 256), acc_t.reshape(NT, 32, 256), cache


def stay(x):
    return pltpu.with_memory_space_constraint(x, pltpu.HBM)


def shards(positions, facing, area, emission, reflect, pair_list):
    held = stay(pair_list.reshape(128, 2).T)
    emission4, reflect4 = stay(emission.reshape(4, 32, 256)), stay(reflect.reshape(4, 32, 256))
    positions, facing, area, emission = stay(positions), stay(facing), stay(area), stay(emission)
    plane = NX * NY * NC
    geo_s, geo_t, w_s, w_t, order = call(
        gather_kernel, 0, (positions, facing, area, emission, held),
        [shape((4 * NS, 24, 256)), shape((NT, 24, 256)), shape((4 * NS, 32, 256), BF16),
         shape((NT, 32, 256), BF16), shape((8, SLOTS + 128), I32)],
        [pltpu.VMEM((3, 16, 256), F32), pltpu.VMEM((2, 16, 256), F32), pltpu.VMEM((16, 256), F32),
         pltpu.VMEM((16, 8, 256), F32), pltpu.VMEM((2, 128), I32), pltpu.SemaphoreType.DMA((5,)),
         pltpu.VMEM((4, 24, 256), F32), pltpu.VMEM((4, 32, 256), BF16), pltpu.VMEM((8, 128), I32),
         pltpu.VMEM((plane, 8, 128), I32), pltpu.VMEM((plane, 128), I32), sems(LINE_GATHER), sems(LINE_GATHER), sems(NS), sems(NS), sems(PLANE_GATHER)],
        "gather", [HBM] * 5,
    )

    quarter = pltpu.VMEM((32, 256), F32)
    landing = [pltpu.VMEM((NX, NY, 32, 256), F32), pltpu.VMEM((PLANE, 32, 256), F32),
               pltpu.VMEM((PLANE, 32, 256), F32), pltpu.VMEM((15, 32, 256), F32),
               pltpu.VMEM((4, 32, 256), F32), pltpu.VMEM((4, 32, 256), F32)]
    acc_s, acc_t, cache = pairs_call(True, order, geo_s, geo_t, w_s, w_t)
    w_s, w_t = call(
        turn_kernel, 1, (acc_s, acc_t, emission4, reflect4, area),
        [shape((4 * NS, 32, 256), BF16), shape((NT, 32, 256), BF16)],
        [quarter, quarter, pltpu.VMEM((16, 256), F32), pltpu.SemaphoreType.DMA((3,))]
        + landing + [pltpu.VMEM((32, 256), BF16), sems(NX), sems(PLANE), sems(LINE_SUM),
                   sems(PLANE_GATHER), sems(LINE_GATHER)],
        "turn", [VMEM, VMEM, HBM, HBM, HBM],
    )
    acc_s, acc_t, _ = pairs_call(False, order, geo_s, geo_t, w_s, w_t, cache)
    (out,) = call(
        last_kernel, 2, (acc_s, acc_t, emission4, reflect4), [shape((4, 32, 256))],
        [quarter, quarter, pltpu.SemaphoreType.DMA((2,))] + landing + [pltpu.VMEM((32, 256), F32), sems(NX), sems(PLANE), sems(LINE_SUM), sems(NY)],
        "last", [VMEM, VMEM, HBM, HBM],
    )
    return out.reshape(16, 8, 256)


def solution(mesh):
    placed = (
        P(None, "pairs", None),
        P(None, "pairs", None),
        P("pairs", None),
        P("pairs", None, None),
        P("pairs", None, None),
        P("pairs", "rep", None, None, None),
    )
    return jax.shard_map(
        shards, mesh=mesh, in_specs=placed, out_specs=P("pairs", None, None), check_vma=False
    )
```
